256 devices in a mesh: row: 16 (over x, y), col: 16 (over z, core).
Axes of the slice: x: 4, y: 4, z: 8, core: 2. Of those that a mesh axis runs over, the one named last changes fastest.
Arguments:
- fresh_queries: bfloat16 [256, 4096], P(('row', 'col')), may hold values from -41.451533 to 41.451533
- fresh_key: bfloat16 [256, 512], P(('row', 'col')), may hold values from -6 to 6
- fresh_value: bfloat16 [256, 512], P(('row', 'col')), may hold values from -8 to 8
- request_own_keys: bfloat16 [256, 512, 512], P(('row', 'col')), may hold values from -4 to 4
- request_own_values: bfloat16 [256, 512, 512], P(('row', 'col')), may hold values from -8 to 8
- leaf_len: int32 [256], P(('row', 'col')), may hold values from 1 to 512, as said below
- prefix_pool_keys: bfloat16 [512, 128, 512], P(('row', 'col')), may hold values from -4 to 4
- prefix_pool_values: bfloat16 [512, 128, 512], P(('row', 'col')), may hold values from -8 to 8
- page_table: int32 [512], replicated, may hold values from 0 to 511, each once
- root_len: int32 [4], replicated, may hold values from 1 to 4096, as said below
- mid_len: int32 [32], replicated, may hold values from 1 to 1536, as said below
- mid_parent: int32 [32], replicated, may hold values from 0 to 3, as said below
- leaf_parent: int32 [256], replicated, may hold values from 0 to 31, as said below
- residual: bfloat16 [256, 2048], P(None, 'row'), may hold values from -3 to 3
- out_weight: bfloat16 [4096, 2048], P('col', 'row'), may hold values from -0.09375 to 0.09375
- post_gain: float32 [2048], P('row'), may hold values from 0.25 to 1.75
- expert_ids: int32 [256, 8], replicated, may hold values from 0 to 127, all different within a row; in each aligned block of 256 rows (0 to 255, 256 to 511, ...) at most 32 rows name the same one
- gate_weight: float32 [256, 8], replicated, may hold values from 0.25 to 1
- w_gate_up: bfloat16 [128, 2048, 1536], P('col', 'row'), may hold values from -0.125 to 0.125
- w_down: bfloat16 [128, 768, 2048], P('col', None, 'row'), may hold values from -0.21875 to 0.21875
Outputs:
- attended: bfloat16 [256, 2048], P(None, 'row')
- layer_out: bfloat16 [256, 2048], P('col', 'row')
The draws below stay inside these ranges and needn't reach their ends.
Inputs may be any that keep to these rules, and one draw needn't show every extreme that they name: `leaf_len`: some request's own cache is full. `root_len`: some root prefix fills all its page slots. `mid_len`: some middle prefix fills all its page slots. `mid_parent`: each root has exactly 8 middle prefixes. `leaf_parent`: each middle prefix has exactly 8 requests. `expert_ids`: each request names 8 different experts; no expert is named by more than 32 requests, a bound that some block reaches.
All inputs are finite; a program needn't handle non-finite values.
Results may differ from the reference program's by a relative error of at most 0.034.
Values may be sent and summed in bfloat16 or wider, within the bound.
A program may use at most 64 MiB of HBM per device.

```python
import math
import jax
import jax.numpy as jnp
import numpy as np
from jax import lax

D = 2048
QUERY_HEADS = 32
KEY_VALUE_HEADS = 4
HEAD_SIZE = 128
EXPERTS = 128
FFE = 768
TOPK = 8
PAGE_POSITIONS = 128
LEAF_REQUESTS = 256
MIDS = 32
ROOTS = 4
ROOT_PAGES = 32
MID_PAGES = 12
LEAF_PAGE_COUNT = 4
CAP = 32
POOL_PAGES = 512
LEAF_LENGTH = 512


def bounded_jitter(key, stream_id, shape):
    return jnp.clip(jax.random.normal(jax.random.fold_in(key, stream_id), shape, jnp.float32), -4.0, 4.0)


def capped_lengths(key, stream_id, entries, longest):
    value_rows = jax.random.randint(jax.random.fold_in(key, stream_id), (entries,), 1, longest + 1)
    peak_at = jax.random.randint(jax.random.fold_in(key, stream_id + 1), (), 0, entries)
    return jnp.where(jnp.arange(entries) == peak_at, longest, value_rows).astype(jnp.int32)


def draw_fresh_queries(key, part):
    random_jitter = bounded_jitter(key, 3, (LEAF_REQUESTS, QUERY_HEADS, HEAD_SIZE))
    value_rows = 2.5 * random_jitter
    return value_rows.reshape(LEAF_REQUESTS, QUERY_HEADS * HEAD_SIZE).astype(jnp.bfloat16)


def draw_prefix_pool_keys(key, part):
    random_jitter = bounded_jitter(key, 1, (POOL_PAGES, PAGE_POSITIONS, KEY_VALUE_HEADS, HEAD_SIZE))
    value_rows = random_jitter
    return value_rows.reshape(POOL_PAGES, PAGE_POSITIONS, KEY_VALUE_HEADS * HEAD_SIZE).astype(jnp.bfloat16)


def draw_request_own_keys(key, part):
    random_jitter = bounded_jitter(key, 2, (LEAF_REQUESTS, LEAF_LENGTH, KEY_VALUE_HEADS, HEAD_SIZE))
    value_rows = random_jitter
    return value_rows.reshape(LEAF_REQUESTS, LEAF_LENGTH, KEY_VALUE_HEADS * HEAD_SIZE).astype(jnp.bfloat16)


def draw_leaf_len(key, part):
    return capped_lengths(key, 41, LEAF_REQUESTS, LEAF_LENGTH)


def draw_root_len(key, part):
    return capped_lengths(key, 43, ROOTS, ROOT_PAGES * PAGE_POSITIONS)


def draw_mid_len(key, part):
    return capped_lengths(key, 45, MIDS, MID_PAGES * PAGE_POSITIONS)


def draw_mid_parent(key, part):
    order = jax.random.permutation(jax.random.fold_in(key, 32), MIDS)
    return (order // (MIDS // ROOTS)).astype(jnp.int32)


def draw_leaf_parent(key, part):
    order = jax.random.permutation(jax.random.fold_in(key, 31), LEAF_REQUESTS)
    return (order // (LEAF_REQUESTS // MIDS)).astype(jnp.int32)


def level_of(stream_key, dims, cuts, low, largest):
    level = 1.0
    for axis_at, parts in cuts:
        draws = jax.random.uniform(jax.random.fold_in(jax.random.fold_in(stream_key, 6), axis_at), (parts,), jnp.float32, low / len(cuts), largest / len(cuts))
        level = level * jnp.repeat(jnp.exp(draws), dims[axis_at] // parts).reshape((-1,) + (1,) * (len(dims) - 1 - axis_at))
    return level


def deal_out(stream_key, own, number, rows, count, top, limit, slope):
    ranking = jax.random.permutation(stream_key, count)
    crowded, common = portions_of(count, rows * top, limit, slope, True), portions_of(count, rows * top, limit, slope, False)
    places = jnp.arange(count)

    def named(sizes, offset_by):
        used = int((sizes > 0).sum())
        fixed = max(1, used // 4)
        shifted = fixed + (places - fixed + offset_by * (used - fixed)) % max(1, count - fixed)
        return jnp.zeros((count,), jnp.int32).at[ranking[jnp.where(places < fixed, places, shifted)]].set(jnp.asarray(sizes, jnp.int32))

    sizes = jnp.where(number % 4 == 0, named(crowded, number // 4), named(common, number - number // 4 - 1))
    mixed = jax.random.permutation(jax.random.fold_in(own, 3), count)
    giver, taker = mixed[0:count // 2 * 2:2], mixed[1:count // 2 * 2:2]
    room = jnp.minimum(sizes[giver] - 1, limit - sizes[taker]) // 2
    room = jnp.where((giver == ranking[0]) | (taker == ranking[0]) | (sizes[taker] == 0), 0, jnp.maximum(room, 0))
    shifted = jax.random.randint(jax.random.fold_in(own, 4), (count // 2,), 0, 1 << 20) % (room + 1)
    sizes = sizes.at[giver].add(-shifted).at[taker].add(shifted)
    items = jnp.searchsorted(jnp.cumsum(sizes), jnp.arange(rows * top), side="right").astype(jnp.int32)
    table = items.reshape(top, rows).T
    table = table[jax.random.permutation(jax.random.fold_in(own, 1), rows)]
    offset_by = jax.random.randint(jax.random.fold_in(own, 2), (rows, 1), 0, top)
    return jnp.take_along_axis(table, (jnp.arange(top)[None, :] + offset_by) % top, axis=1)


def portions_of(amount, total, most, skew, full):
    portions = [(1 << 20) // math.isqrt(standing ** skew) + 1 for standing in range(1, amount + 1)]
    largest = most if full else min(most, max(-(-total // amount), total * portions[0] // sum(portions)))
    least = 1 if total - largest >= amount - 1 else 0
    given, surplus = [largest] + [least] * (amount - 1), total - largest - least * (amount - 1)
    while surplus > 0:
        candidates = [i for i in range(1, amount) if given[i] < largest] or [i for i in range(1, amount) if given[i] < most]
        pool, budget = sum([portions[i] for i in candidates]), surplus
        for i in candidates:
            addition = min(most - given[i], max(1, budget * portions[i] // pool), surplus)
            given[i] = given[i] + addition
            surplus = surplus - addition
    return np.array(given)


def centred(rng, shape, scale, limit, shards=(), kind=jnp.bfloat16):
    values = scale * jax.random.normal(rng, shape, jnp.float32)
    if shards:
        values = values * level_of(rng, shape, shards, -0.22, 0.18)
    return jnp.clip(values, -limit, limit).astype(kind)


def setup_inputs(seed: int = 0) -> dict:
    key_list = jax.random.split(jax.random.key(seed), 21)
    fresh_queries = draw_fresh_queries(jax.random.fold_in(key_list[20], 71), 0)
    fresh_key = centred(key_list[1], (LEAF_REQUESTS, KEY_VALUE_HEADS * HEAD_SIZE), 1.6, 6.0, ((0, 256),))
    fresh_value = centred(key_list[2], (LEAF_REQUESTS, KEY_VALUE_HEADS * HEAD_SIZE), 2.0, 8.0, ((0, 256),))
    request_own_keys = draw_request_own_keys(jax.random.fold_in(key_list[20], 71), 0)
    request_own_values = centred(key_list[4], (LEAF_REQUESTS, LEAF_LENGTH, KEY_VALUE_HEADS * HEAD_SIZE), 2.0, 8.0, ((0, 256),))
    leaf_len = draw_leaf_len(jax.random.fold_in(key_list[20], 71), 0)
    prefix_pool_keys = draw_prefix_pool_keys(jax.random.fold_in(key_list[20], 71), 0)
    prefix_pool_values = centred(key_list[7], (POOL_PAGES, PAGE_POSITIONS, KEY_VALUE_HEADS * HEAD_SIZE), 2.0, 8.0, ((0, 256),))
    page_table = jax.random.permutation(key_list[8], POOL_PAGES).astype(jnp.int32)
    root_len = draw_root_len(jax.random.fold_in(key_list[20], 71), 0)
    mid_len = draw_mid_len(jax.random.fold_in(key_list[20], 71), 0)
    mid_parent = draw_mid_parent(jax.random.fold_in(key_list[20], 71), 0)
    leaf_parent = draw_leaf_parent(jax.random.fold_in(key_list[20], 71), 0)
    residual = centred(key_list[13], (LEAF_REQUESTS, D), 0.5, 3.0, ((1, 16),))
    out_weight = centred(key_list[14], (QUERY_HEADS * HEAD_SIZE, D), (QUERY_HEADS * HEAD_SIZE) ** -0.5, 0.09375, ((0, 16), (1, 16)))
    post_gain = jnp.clip(1.0 + 0.15 * jax.random.normal(key_list[15], (D,), jnp.float32), 0.25, 1.75)
    expert_ids_keys = jax.random.split(jax.random.fold_in(key_list[16], 1), LEAF_REQUESTS // LEAF_REQUESTS)
    expert_ids_turns = jax.random.permutation(jax.random.fold_in(key_list[16], 3), LEAF_REQUESTS // LEAF_REQUESTS)
    expert_ids = jax.vmap(lambda own, number: deal_out(jax.random.fold_in(key_list[16], 2), own, number, LEAF_REQUESTS, EXPERTS, TOPK, CAP, 1))(expert_ids_keys, expert_ids_turns).reshape((LEAF_REQUESTS, TOPK))
    gate_weight = jnp.clip(jax.random.uniform(key_list[17], (LEAF_REQUESTS, TOPK), jnp.float32, 0.25, 1.0), 0.25, 1.0)
    w_gate_up = centred(key_list[18], (EXPERTS, D, 2 * FFE), D ** -0.5, 0.125, ((0, 16), (1, 16)))
    w_down = centred(key_list[19], (EXPERTS, FFE, D), FFE ** -0.5, 0.21875, ((0, 16), (2, 16)))
    return dict(fresh_queries=fresh_queries, fresh_key=fresh_key, fresh_value=fresh_value, request_own_keys=request_own_keys, request_own_values=request_own_values, leaf_len=leaf_len, prefix_pool_keys=prefix_pool_keys, prefix_pool_values=prefix_pool_values, page_table=page_table, root_len=root_len, mid_len=mid_len, mid_parent=mid_parent, leaf_parent=leaf_parent, residual=residual, out_weight=out_weight, post_gain=post_gain, expert_ids=expert_ids, gate_weight=gate_weight, w_gate_up=w_gate_up, w_down=w_down)


NEG = -1e+30
EPS = 1e-06

def block_parts(score_rows, living_mask, value_rows, form):
    masked = jnp.where(living_mask, score_rows, NEG)
    block_peak = lax.optimization_barrier(jnp.max(masked, axis=-1))
    weights = jnp.where(living_mask, jnp.exp(masked - block_peak[..., None]), 0.0)
    block_mass = lax.optimization_barrier(jnp.sum(weights, axis=-1))
    rounded = weights.astype(jnp.bfloat16).astype(jnp.float32)
    block_sum = jnp.einsum(form, rounded, value_rows.astype(jnp.float32))
    return (block_peak, block_mass, block_sum)

def reference(fresh_queries, fresh_key, fresh_value, request_own_keys, request_own_values, leaf_len, prefix_pool_keys, prefix_pool_values, page_table, root_len, mid_len, mid_parent, leaf_parent, residual, out_weight, post_gain, expert_ids, gate_weight, w_gate_up, w_down):
    query_group_width = QUERY_HEADS // KEY_VALUE_HEADS
    score_factor = 1.0 / math.sqrt(HEAD_SIZE)
    mid_ids = jnp.arange(MIDS, dtype=jnp.int32)
    request_root = lax.optimization_barrier(jnp.sum(jnp.where(leaf_parent[:, None] == mid_ids[None, :], mid_parent[None, :], 0), axis=1)).astype(jnp.int32)
    first_mid = ROOTS * ROOT_PAGES

    def prefix_blocks(query_vector, first_slot, page_list, length):
        page_numbers = lax.dynamic_slice_in_dim(page_table, first_slot, page_list)
        key_rows = prefix_pool_keys[page_numbers].reshape(page_list, PAGE_POSITIONS, KEY_VALUE_HEADS, HEAD_SIZE)
        value_rows = prefix_pool_values[page_numbers].reshape(page_list, PAGE_POSITIONS, KEY_VALUE_HEADS, HEAD_SIZE)
        score_rows = jnp.einsum('kgd,npkd->nkgp', query_vector.astype(jnp.float32), key_rows.astype(jnp.float32)) * score_factor
        positions = jnp.arange(page_list, dtype=jnp.int32)[:, None] * PAGE_POSITIONS + jnp.arange(PAGE_POSITIONS, dtype=jnp.int32)[None, :]
        living_mask = (positions < length)[:, None, None, :]
        peaks, masses, sums = block_parts(score_rows, living_mask, value_rows, 'nkgp,npkd->nkgd')
        return (peaks.reshape(page_list, QUERY_HEADS), masses.reshape(page_list, QUERY_HEADS), sums.reshape(page_list, QUERY_HEADS, HEAD_SIZE))

    def one_request(request_index):
        query_vector = fresh_queries[request_index].reshape(KEY_VALUE_HEADS, query_group_width, HEAD_SIZE)
        root = request_root[request_index]
        middle = leaf_parent[request_index]
        root_parts = prefix_blocks(query_vector, (root * ROOT_PAGES).astype(jnp.int32), ROOT_PAGES, root_len[root])
        mid_parts = prefix_blocks(query_vector, (first_mid + middle * MID_PAGES).astype(jnp.int32), MID_PAGES, mid_len[middle])
        key_rows = request_own_keys[request_index].reshape(LEAF_PAGE_COUNT, PAGE_POSITIONS, KEY_VALUE_HEADS, HEAD_SIZE)
        value_rows = request_own_values[request_index].reshape(LEAF_PAGE_COUNT, PAGE_POSITIONS, KEY_VALUE_HEADS, HEAD_SIZE)
        score_rows = jnp.einsum('kgd,npkd->nkgp', query_vector.astype(jnp.float32), key_rows.astype(jnp.float32)) * score_factor
        positions = jnp.arange(LEAF_PAGE_COUNT, dtype=jnp.int32)[:, None] * PAGE_POSITIONS + jnp.arange(PAGE_POSITIONS, dtype=jnp.int32)[None, :]
        living_mask = (positions < leaf_len[request_index])[:, None, None, :]
        peaks, masses, sums = block_parts(score_rows, living_mask, value_rows, 'nkgp,npkd->nkgd')
        leaf_parts = (peaks.reshape(LEAF_PAGE_COUNT, QUERY_HEADS), masses.reshape(LEAF_PAGE_COUNT, QUERY_HEADS), sums.reshape(LEAF_PAGE_COUNT, QUERY_HEADS, HEAD_SIZE))
        fresh_token_score = jnp.einsum('pso,po->ps', query_vector.astype(jnp.float32), fresh_key[request_index].reshape(KEY_VALUE_HEADS, HEAD_SIZE).astype(jnp.float32)) * score_factor
        fresh_token_value = jnp.broadcast_to(fresh_value[request_index].reshape(KEY_VALUE_HEADS, 1, HEAD_SIZE).astype(jnp.float32), (KEY_VALUE_HEADS, query_group_width, HEAD_SIZE)).reshape(1, QUERY_HEADS, HEAD_SIZE)
        new_parts = (fresh_token_score.reshape(1, QUERY_HEADS), jnp.ones((1, QUERY_HEADS), jnp.float32), fresh_token_value)
        all_peaks = jnp.concatenate([root_parts[0], mid_parts[0], leaf_parts[0], new_parts[0]], axis=0)
        all_mass = jnp.concatenate([root_parts[1], mid_parts[1], leaf_parts[1], new_parts[1]], axis=0)
        all_sums = jnp.concatenate([root_parts[2], mid_parts[2], leaf_parts[2], new_parts[2]], axis=0)
        overall = lax.optimization_barrier(jnp.max(all_peaks, axis=0))
        factor = jnp.exp(all_peaks - overall[None, :])
        mass = lax.optimization_barrier(jnp.sum(factor * all_mass, axis=0))
        summed = lax.optimization_barrier(jnp.sum(factor[:, :, None] * all_sums, axis=0))
        return (summed / mass[:, None]).astype(jnp.bfloat16).reshape(QUERY_HEADS * HEAD_SIZE)
    attn = lax.map(one_request, jnp.arange(LEAF_REQUESTS, dtype=jnp.int32))
    projected = jnp.dot(attn, out_weight, preferred_element_type=jnp.float32)
    attended = (residual.astype(jnp.float32) + projected).astype(jnp.bfloat16)
    squares = lax.optimization_barrier(jnp.sum(jnp.square(attended.astype(jnp.float32)), axis=1))
    inverse = lax.rsqrt(squares / D + EPS)
    scaled = (attended * post_gain).astype(jnp.bfloat16)
    request_ids = jnp.arange(LEAF_REQUESTS, dtype=jnp.int32)
    slot_ids = jnp.arange(CAP, dtype=jnp.int32)

    def expert_step(carried, item):
        index, gate_up_weight, down_weight = item
        names_it = expert_ids == index
        chosen_by = jnp.any(names_it, axis=1)
        weight_of = lax.optimization_barrier(jnp.sum(jnp.where(names_it, gate_weight, 0.0), axis=1))
        slot_rank = jnp.cumsum(chosen_by.astype(jnp.int32)) - 1
        slot_hit = chosen_by[:, None] & (slot_rank[:, None] == slot_ids[None, :])
        token_of = lax.optimization_barrier(jnp.sum(jnp.where(slot_hit, request_ids[:, None], 0), axis=0)).astype(jnp.int32)
        slot_weight = lax.optimization_barrier(jnp.sum(jnp.where(slot_hit, weight_of[:, None], 0.0), axis=0))
        rows_in = scaled[token_of]
        gate_up = jnp.dot(rows_in, gate_up_weight, preferred_element_type=jnp.float32) * inverse[token_of][:, None]
        activated = (jax.nn.silu(gate_up[:, :FFE]) * gate_up[:, FFE:]).astype(jnp.bfloat16)
        expert_out = jnp.dot(activated, down_weight, preferred_element_type=jnp.float32) * slot_weight[:, None]
        return (carried.at[token_of].add(expert_out), None)
    mixed, _ = lax.scan(expert_step, jnp.zeros((LEAF_REQUESTS, D), jnp.float32), (jnp.arange(EXPERTS, dtype=jnp.int32), w_gate_up, w_down))
    layer_out = (attended.astype(jnp.float32) + mixed).astype(jnp.bfloat16)
    return (attended, layer_out)
```

```python
import functools
import math

import jax
import jax.numpy as jnp
from jax import lax
from jax.experimental import pallas as pl
from jax.experimental.pallas import tpu as pltpu
from jax.sharding import PartitionSpec as P

D = 2048
HEAD = 128
FFE = 768
ROOTS = 4
MIDS = 32
ROOT_PAGES = 32
MID_PAGES = 12
N = 16
TOKENS = 256
CAP = 32
EXPERTS_HERE = 8
WIDE = 2 * FFE + 128
EPS = 1e-06
DEAD = -float(2**99)
LOG2E = math.log2(math.e)
SCORE = LOG2E / math.sqrt(HEAD)
MESH = pl.DeviceIdType.MESH
F32 = jnp.float32
BF16 = jnp.bfloat16


def dot(a, b):
    return jnp.dot(a, b, preferred_element_type=F32)


def dot_nt(a, b):
    return lax.dot_general(a, b, (((1,), (1,)), ((), ())), preferred_element_type=F32)


def iota(shape, axis):
    return lax.broadcasted_iota(jnp.int32, shape, axis)


def kernel(
    q_ref,
    fk_ref,
    fv_ref,
    ownk_hbm,
    ownv_hbm,
    leaf_len,
    pk_hbm,
    pv_hbm,
    pt_ref,
    root_len,
    mid_len,
    mid_parent,
    lp_ref,
    resid_ref,
    ow_ref,
    gain_ref,
    ids_ref,
    gw_ref,
    wgu_hbm,
    wdn_hbm,
    att_ref,
    lay_ref,
    ownk,
    ownv,
    wgu,
    wdn,
    kbuf,
    vbuf,
    vt,
    lb,
    wb,
    q1buf,
    qblk,
    sacc,
    racc,
    msg,
    rmsg,
    lsend,
    lrecv,
    attnb,
    psend,
    precv,
    attb,
    disp,
    dispt,
    slotw,
    rin,
    gsend,
    grecv,
    actb,
    yb,
    msend,
    mrecv,
    loc_sem,
    kv_s,
    kv_r,
    q1_s,
    q1_r,
    q2_s,
    q2_r,
    ac_s,
    ac_r,
    ms_s,
    ms_r,
    lf_s,
    lf_r,
    an_s,
    an_r,
    pr_s,
    pr_r,
    at_s,
    at_r,
    gu_s,
    gu_r,
    av_s,
    av_r,
    mx_s,
    mx_r,
):
    r = lax.axis_index("row")
    c = lax.axis_index("col")
    z = c // 2
    core = lax.rem(c, 2)
    kv = lax.rem(z, 4)

    def remote(src, dst, ssem, rsem, dev):
        return pltpu.make_async_remote_copy(
            src_ref=src, dst_ref=dst, send_sem=ssem, recv_sem=rsem, device_id=dev, device_id_type=MESH
        )

    def row_mate(i):
        return lax.rem(c + i, N)

    def col_mate(i):
        return lax.rem(r + i, N)

    lanes = pl.ds(pl.multiple_of(kv * HEAD, HEAD), HEAD)
    own_k = pltpu.make_async_copy(pk_hbm.at[:, :, lanes], kbuf.at[pl.ds(0, 2)], loc_sem.at[0])
    own_v = pltpu.make_async_copy(pv_hbm.at[:, :, lanes], vbuf.at[pl.ds(0, 2)], loc_sem.at[1])
    leaf_k = pltpu.make_async_copy(ownk_hbm, ownk, loc_sem.at[2])
    leaf_v = pltpu.make_async_copy(ownv_hbm, ownv, loc_sem.at[3])
    load_gu = pltpu.make_async_copy(wgu_hbm, wgu, loc_sem.at[4])
    load_dn = pltpu.make_async_copy(wdn_hbm, wdn, loc_sem.at[5])
    own_k.start()
    own_v.start()
    leaf_k.start()
    leaf_v.start()

    barrier = pltpu.get_barrier_semaphore()

    def greet(i, carry):
        pl.semaphore_signal(barrier, inc=1, device_id=(r, row_mate(i)), device_id_type=MESH)
        pl.semaphore_signal(barrier, inc=1, device_id=(col_mate(i), c), device_id_type=MESH)
        return carry

    lax.fori_loop(1, N, greet, 0)
    pl.semaphore_wait(barrier, 2 * (N - 1))

    def q1_copy(i):
        to = row_mate(i)
        head = lax.rem(to // 2, 4)
        return remote(q_ref.at[head], q1buf.at[c], q1_s.at[i], q1_r.at[c], (r, to))

    def q1_start(i, carry):
        q1_copy(i).start()
        return carry

    lax.fori_loop(1, N, q1_start, 0)

    def kv_copies():
        out = []
        for which, (src, dst) in enumerate(((pk_hbm, kbuf), (pv_hbm, vbuf))):
            for j, (step, pages, slot) in enumerate(
                ((1, (0, 2), 2), (7, (0, 2), 4), (2, (0, 1), 6), (6, (1, 1), 7))
            ):
                zt = lax.rem(z + step, 8)
                there = pl.ds(pl.multiple_of(lax.rem(zt, 4) * HEAD, HEAD), HEAD)
                out.append(
                    remote(
                        src.at[pl.ds(*pages), :, there],
                        dst.at[pl.ds(slot, pages[1])],
                        kv_s.at[which * 4 + j],
                        kv_r.at[which * 4 + j],
                        (r, zt * 2 + core),
                    )
                )
        return out

    kv_list = kv_copies()
    for cp in kv_list:
        cp.start()
    load_gu.start()
    load_dn.start()
    q1buf[c] = q_ref[kv]

    lp = lp_ref[...]
    root_of = jnp.zeros((1, TOKENS), jnp.int32)
    for m in range(MIDS):
        root_of = jnp.where(lp == m, mid_parent[m], root_of)
    slot8 = iota((8, 1), 0)
    from_z = jnp.where(
        slot8 < 2,
        z,
        jnp.where(
            slot8 < 4,
            lax.rem(z + 7, 8),
            jnp.where(slot8 < 6, lax.rem(z + 1, 8), jnp.where(slot8 == 6, lax.rem(z + 6, 8), lax.rem(z + 2, 8))),
        ),
    )
    page_of = jnp.where(slot8 < 6, jnp.bitwise_and(slot8, 1), slot8 - 6)
    page_id = 2 * (r * N + 2 * from_z + core) + page_of
    place = jnp.sum(
        jnp.where(pt_ref[...] == page_id, iota((8, 512), 1), 0).astype(F32), axis=1, keepdims=True
    ).astype(jnp.int32)
    owner = jnp.zeros((8, 1), jnp.int32)
    first = jnp.zeros((8, 1), jnp.int32)
    length = jnp.zeros((8, 1), jnp.int32)
    root_slots = ROOTS * ROOT_PAGES
    for m in range(ROOTS):
        hit = (place >= m * ROOT_PAGES) & (place < (m + 1) * ROOT_PAGES)
        owner = jnp.where(hit, m, owner)
        first = jnp.where(hit, m * ROOT_PAGES, first)
        length = jnp.where(hit, root_len[m], length)
    for m in range(MIDS):
        lo = root_slots + m * MID_PAGES
        hit = (place >= lo) & (place < lo + MID_PAGES)
        owner = jnp.where(hit, m, owner)
        first = jnp.where(hit, lo, first)
        length = jnp.where(hit, mid_len[m], length)
    alive = length - (place - first) * HEAD
    owned = jnp.where(place < root_slots, root_of, lp) == owner
    owned = jnp.where(owned, 1.0, 0.0)
    spread = jnp.concatenate([owned] * N, axis=0)
    spread = jnp.where(iota((128, TOKENS), 0) // 8 == iota((128, TOKENS), 1) // N, spread, 0.0)
    fold = jnp.where(lax.rem(iota((TOKENS, 128), 0), N) == lax.rem(iota((TOKENS, 128), 1), N), 1.0, 0.0)
    wb[...] = (1.0 - dot(spread.astype(BF16), fold.astype(BF16))) * DEAD
    for p in range(8):
        limit = jnp.broadcast_to(alive[p : p + 1, :], (128, 128))
        lb[pl.ds(p * 128, 128), :] = jnp.where(iota((128, 128), 0) < limit, 0.0, DEAD)

    def q1_wait(i, carry):
        src = row_mate(i)
        remote(q_ref.at[0], q1buf.at[src], q1_s.at[i], q1_r.at[src], (r, src)).wait_recv()
        return carry

    lax.fori_loop(1, N, q1_wait, 0)
    order = jnp.where(
        iota((128, 128), 1) == lax.rem(iota((128, 128), 0), N) * 8 + iota((128, 128), 0) // N, 1.0, 0.0
    ).astype(BF16)
    qblk[r] = dot(order, q1buf[...].reshape(128, HEAD)).astype(BF16)

    def q2_copy(i):
        to = col_mate(i)
        return remote(qblk.at[r], qblk.at[r], q2_s.at[i], q2_r.at[r], (to, c))

    def q2_start(i, carry):
        q2_copy(i).start()
        return carry

    lax.fori_loop(1, N, q2_start, 0)

    leaf_k.wait()
    leaf_v.wait()
    for k in range(4):
        q8 = q_ref[k]
        s = dot_nt(q8, ownk[0, :, k * HEAD : (k + 1) * HEAD]) * SCORE
        s = jnp.where(iota((8, 512), 1) < leaf_len[0], s, DEAD)
        fresh = jnp.sum(q8.astype(F32) * fk_ref[k : k + 1, :].astype(F32), axis=1, keepdims=True) * SCORE
        m = jnp.maximum(jnp.max(s, axis=1, keepdims=True), fresh)
        p = jnp.exp2(s - m)
        pf = jnp.exp2(fresh - m)
        total = jnp.sum(p, axis=1, keepdims=True) + pf
        acc = dot(p.astype(BF16), ownv[0, :, k * HEAD : (k + 1) * HEAD]) + pf * fv_ref[k : k + 1, :].astype(F32)
        m = jnp.broadcast_to(m, (8, HEAD))
        total = jnp.broadcast_to(total, (8, HEAD))
        for j in range(4):
            two = slice(2 * j, 2 * j + 2)
            lsend[4 * k + j] = jnp.concatenate([acc[two], m[two], total[two], total[two]], axis=0)

    def leaf_copy(i):
        to = row_mate(i)
        return remote(lsend.at[to], lrecv.at[c], lf_s.at[i], lf_r.at[c], (r, to))

    def leaf_start(i, carry):
        leaf_copy(i).start()
        return carry

    lax.fori_loop(1, N, leaf_start, 0)
    lrecv[c] = lsend[c]

    own_k.wait()
    own_v.wait()
    for cp in kv_list:
        cp.wait_recv()
    for p in range(8):
        vt[:, p * 128 : (p + 1) * 128] = vbuf[p].astype(F32).T.astype(BF16)

    def acc_copy(i):
        to = col_mate(i)
        return remote(sacc.at[to], racc.at[r], ac_s.at[i], ac_r.at[r], (to, c))

    def attend(i, carry):
        b = col_mate(i)

        @pl.when(i > 0)
        def _():
            remote(qblk.at[r], qblk.at[b], q2_s.at[i], q2_r.at[b], (b, c)).wait_recv()

        s = dot_nt(kbuf[...].reshape(1024, HEAD), qblk[b]) * SCORE + lb[...]
        bias = wb[pl.ds(pl.multiple_of(b * 8, 8), 8), :]
        s = (s.reshape(8, 128, 128) + bias[:, None, :]).reshape(1024, 128)
        m = jnp.max(s, axis=0, keepdims=True).astype(BF16).astype(F32)
        p = jnp.exp2(s - m)
        total = jnp.sum(p, axis=0, keepdims=True)
        hi = total.astype(BF16).astype(F32)
        row = iota((16, 128), 0)
        tail = jnp.where(row == 0, m, jnp.where(row == 1, hi, jnp.where(row == 2, total - hi, 0.0)))
        sacc[b, 0:128, :] = dot(vt[...], p.astype(BF16)).astype(BF16)
        sacc[b, 128:144, :] = tail.astype(BF16)

        @pl.when(i > 0)
        def _():
            acc_copy(i).start()

        return carry

    lax.fori_loop(0, N, attend, 0)

    ids = ids_ref[...]
    gw = gw_ref[...]
    chosen, weight = [], []
    for e in range(EXPERTS_HERE):
        hit = ids == c * EXPERTS_HERE + e
        chosen.append(jnp.max(jnp.where(hit, 1.0, 0.0), axis=0, keepdims=True))
        weight.append(jnp.sum(jnp.where(hit, gw, 0.0), axis=0, keepdims=True))
    picks = jnp.concatenate(chosen, axis=0)
    upto = jnp.where(iota((TOKENS, TOKENS), 0) <= iota((TOKENS, TOKENS), 1), 1.0, 0.0).astype(BF16)
    rank = dot(picks.astype(BF16), upto) - 1.0
    for e in range(EXPERTS_HERE):
        slot = iota((CAP, TOKENS), 0).astype(F32)
        one = jnp.where((rank[e : e + 1, :] == slot) & (picks[e : e + 1, :] > 0.5), 1.0, 0.0)
        disp[e * CAP : (e + 1) * CAP, :] = one.astype(BF16)
        slotw[e * CAP : (e + 1) * CAP, :] = jnp.broadcast_to(
            jnp.sum(one * weight[e], axis=1, keepdims=True), (CAP, 128)
        )
    dispt[...] = disp[...].astype(F32).T.astype(BF16)

    racc[r] = sacc[r]

    def acc_wait(i, top):
        src = col_mate(i)
        remote(sacc.at[r], racc.at[src], ac_s.at[i], ac_r.at[src], (src, c)).wait_recv()
        return jnp.maximum(top, racc[src, 128:144, :].astype(F32)[0:1, :])

    top = lax.fori_loop(1, N, acc_wait, racc[r, 128:144, :].astype(F32)[0:1, :])

    def acc_add(i, carry):
        acc, total = carry
        tail = racc[i, 128:144, :].astype(F32)
        f = jnp.exp2(tail[0:1, :] - top)
        return acc + racc[i, 0:128, :].astype(F32) * f, total + (tail[1:2, :] + tail[2:3, :]) * f

    acc, total = lax.fori_loop(0, N, acc_add, (jnp.zeros((128, 128), F32), jnp.zeros((1, 128), F32)))
    hi = total.astype(BF16).astype(F32)
    row = iota((128, 128), 0)
    tail = jnp.where(row == 0, top, jnp.where(row == 1, hi, jnp.where(row == 2, total - hi, 0.0)))
    msg[:, :, 0:128] = acc.T.astype(BF16).reshape(4, 32, 128)
    msg[:, :, 128:256] = tail.T.astype(BF16).reshape(4, 32, 128)
    here = z // 4 * 2 + core

    for j in range(4):
        to = 4 * kv + j

        @pl.when(to != c)
        def _():
            remote(msg.at[j], rmsg.at[here], ms_s.at[j], ms_r.at[here], (r, to)).start()

        @pl.when(to == c)
        def _():
            pltpu.make_async_copy(msg.at[j], rmsg.at[here], ms_r.at[here]).start()

    def leaf_wait(i, carry):
        src = row_mate(i)
        remote(lsend.at[0], lrecv.at[src], lf_s.at[i], lf_r.at[src], (r, src)).wait_recv()
        return carry

    lax.fori_loop(1, N, leaf_wait, 0)
    leaf_acc = jnp.concatenate([lrecv[:, 0, :], lrecv[:, 1, :]], axis=0)
    leaf_m = jnp.concatenate([lrecv[:, 2, :], lrecv[:, 3, :]], axis=0)
    leaf_t = jnp.concatenate([lrecv[:, 4, :], lrecv[:, 5, :]], axis=0)
    for s in range(4):
        pltpu.make_async_copy(msg.at[0], rmsg.at[s], ms_r.at[s]).wait()
    parts = []
    top = leaf_m
    for s in range(4):
        tail = rmsg[s, :, 128:256].astype(F32)
        m = jnp.broadcast_to(tail[:, 0:1], (32, 128))
        parts.append((m, tail[:, 1:2] + tail[:, 2:3], rmsg[s, :, 0:128].astype(F32)))
        top = jnp.maximum(top, m)
    f = jnp.exp2(leaf_m - top)
    acc, total = leaf_acc * f, leaf_t * f
    for m, t, a in parts:
        f = jnp.exp2(m - top)
        acc = acc + a * f
        total = total + t * f
    attnb[r] = (acc / total).astype(BF16)

    def an_copy(i):
        to = col_mate(i)
        return remote(attnb.at[r], attnb.at[r], an_s.at[i], an_r.at[r], (to, c))

    def an_start(i, carry):
        an_copy(i).start()
        return carry

    lax.fori_loop(1, N, an_start, 0)

    def an_wait(i, carry):
        src = col_mate(i)
        remote(attnb.at[r], attnb.at[src], an_s.at[i], an_r.at[src], (src, c)).wait_recv()
        return carry

    lax.fori_loop(1, N, an_wait, 0)

    proj = dot(attnb[:, 0:16, :].reshape(TOKENS, HEAD), ow_ref[0:HEAD, :])
    proj = proj + dot(attnb[:, 16:32, :].reshape(TOKENS, HEAD), ow_ref[HEAD : 2 * HEAD, :])
    psend[...] = proj.astype(BF16).reshape(N, 16, 128)

    def pr_copy(i):
        to = row_mate(i)
        return remote(psend.at[to], precv.at[c], pr_s.at[i], pr_r.at[c], (r, to))

    def pr_start(i, carry):
        pr_copy(i).start()
        return carry

    lax.fori_loop(1, N, pr_start, 0)
    precv[c] = psend[c]

    def pr_wait(i, carry):
        src = row_mate(i)
        remote(psend.at[0], precv.at[src], pr_s.at[i], pr_r.at[src], (r, src)).wait_recv()
        return carry

    lax.fori_loop(1, N, pr_wait, 0)
    mine = pl.ds(pl.multiple_of(c * 16, 16), 16)
    own_att = resid_ref[mine, :].astype(F32) + jnp.sum(precv[...].astype(F32), axis=0)
    attb[c] = own_att.astype(BF16)

    def at_copy(i):
        to = row_mate(i)
        return remote(attb.at[c], attb.at[c], at_s.at[i], at_r.at[c], (r, to))

    def at_start(i, carry):
        at_copy(i).start()
        return carry

    lax.fori_loop(1, N, at_start, 0)

    def at_wait(i, carry):
        src = row_mate(i)
        remote(attb.at[c], attb.at[src], at_s.at[i], at_r.at[src], (r, src)).wait_recv()
        return carry

    lax.fori_loop(1, N, at_wait, 0)
    att = attb[...].reshape(TOKENS, 128)
    att_ref[...] = att

    wide = att.astype(F32)
    squares = jnp.sum(wide * wide, axis=1, keepdims=True)
    hi = squares.astype(BF16).astype(F32)
    lane = iota((TOKENS, 128), 1)
    side = jnp.where(lane == 0, hi, jnp.where(lane == 1, squares - hi, 0.0))
    scaled = (wide * gain_ref[...]).astype(BF16)
    rin[...] = dot(disp[...], jnp.concatenate([scaled, side.astype(BF16)], axis=1)).astype(BF16)
    load_gu.wait()

    def gu_copy(to):
        return remote(gsend.at[to], grecv.at[r], gu_s.at[to], gu_r.at[r], (to, c))

    def gate_up(i, carry):
        e = lax.rem(r // 2 + i, EXPERTS_HERE)
        rows = rin[pl.ds(pl.multiple_of(e * CAP, CAP), CAP), :]
        part = dot(rows[:, 0:128], wgu[e]).astype(BF16)
        for half in range(2):
            to = 2 * e + half
            cut = slice(16 * half, 16 * half + 16)
            gsend[to, :, 0 : 2 * FFE] = part[cut, :]
            gsend[to, :, 2 * FFE : WIDE] = rows[cut, 128:256]

            @pl.when(to != r)
            def _():
                gu_copy(to).start()

        return carry

    lax.fori_loop(0, EXPERTS_HERE, gate_up, 0)
    grecv[r] = gsend[r]

    def gu_wait(i, carry):
        src = col_mate(i)
        remote(gsend.at[r], grecv.at[src], gu_s.at[0], gu_r.at[src], (src, c)).wait_recv()
        return carry

    lax.fori_loop(1, N, gu_wait, 0)

    def gu_add(i, acc):
        return acc + grecv[i].astype(F32)

    gu = lax.fori_loop(0, N, gu_add, jnp.zeros((16, WIDE), F32))
    inverse = lax.rsqrt((gu[:, 2 * FFE : 2 * FFE + 1] + gu[:, 2 * FFE + 1 : 2 * FFE + 2]) / D + EPS)
    gate = gu[:, 0:FFE] * inverse
    up = gu[:, FFE : 2 * FFE] * inverse
    actb[r] = (gate / (1.0 + jnp.exp(-gate)) * up).astype(BF16)

    def av_copy(i):
        to = col_mate(i)
        return remote(actb.at[r], actb.at[r], av_s.at[i], av_r.at[r], (to, c))

    def av_start(i, carry):
        av_copy(i).start()
        return carry

    lax.fori_loop(1, N, av_start, 0)
    load_dn.wait()

    def av_wait(i, carry):
        src = col_mate(i)
        remote(actb.at[r], actb.at[src], av_s.at[i], av_r.at[src], (src, c)).wait_recv()
        return carry

    lax.fori_loop(1, N, av_wait, 0)

    def down(e, carry):
        rows = actb[pl.ds(2 * e, 2)].reshape(CAP, FFE)
        at = pl.ds(pl.multiple_of(e * CAP, CAP), CAP)
        y = dot(rows, wdn[e]) * slotw[at, :]
        hi = y.astype(BF16)
        yb[at, 0:128] = hi
        yb[at, 128:256] = (y - hi.astype(F32)).astype(BF16)
        return carry

    lax.fori_loop(0, EXPERTS_HERE, down, 0)
    mixed = dot(dispt[...], yb[...])
    msend[...] = (mixed[:, 0:128] + mixed[:, 128:256]).astype(BF16).reshape(N, 16, 128)

    def mx_copy(i):
        to = row_mate(i)
        return remote(msend.at[to], mrecv.at[c], mx_s.at[i], mx_r.at[c], (r, to))

    def mx_start(i, carry):
        mx_copy(i).start()
        return carry

    lax.fori_loop(1, N, mx_start, 0)
    mrecv[c] = msend[c]

    def mx_wait(i, carry):
        src = row_mate(i)
        remote(msend.at[0], mrecv.at[src], mx_s.at[i], mx_r.at[src], (r, src)).wait_recv()
        return carry

    lax.fori_loop(1, N, mx_wait, 0)
    lay_ref[...] = (attb[c].astype(F32) + jnp.sum(mrecv[...].astype(F32), axis=0)).astype(BF16)

    for cp in kv_list:
        cp.wait_send()

    def drain(i, carry):
        q1_copy(i).wait_send()
        q2_copy(i).wait_send()
        leaf_copy(i).wait_send()
        acc_copy(i).wait_send()
        an_copy(i).wait_send()
        pr_copy(i).wait_send()
        at_copy(i).wait_send()
        gu_copy(col_mate(i)).wait_send()
        av_copy(i).wait_send()
        mx_copy(i).wait_send()
        return carry

    lax.fori_loop(1, N, drain, 0)
    for j in range(4):
        to = 4 * kv + j

        @pl.when(to != c)
        def _():
            remote(msg.at[j], rmsg.at[here], ms_s.at[j], ms_r.at[here], (r, to)).wait_send()


def per_device(
    fresh_queries,
    fresh_key,
    fresh_value,
    request_own_keys,
    request_own_values,
    leaf_len,
    prefix_pool_keys,
    prefix_pool_values,
    page_table,
    root_len,
    mid_len,
    mid_parent,
    leaf_parent,
    residual,
    out_weight,
    post_gain,
    expert_ids,
    gate_weight,
    w_gate_up,
    w_down,
):
    vmem = pl.BlockSpec(memory_space=pltpu.VMEM)
    smem = pl.BlockSpec(memory_space=pltpu.SMEM)
    anys = pl.BlockSpec(memory_space=pl.ANY)
    dma = lambda n: pltpu.SemaphoreType.DMA((n,))
    return pl.pallas_call(
        kernel,
        out_shape=(
            jax.ShapeDtypeStruct((TOKENS, 128), BF16),
            jax.ShapeDtypeStruct((16, 128), BF16),
        ),
        in_specs=[
            vmem, vmem, vmem, anys, anys, smem, anys, anys, vmem, smem, smem, smem, vmem,
            vmem, vmem, vmem, vmem, vmem, anys, anys,
        ],
        out_specs=(vmem, vmem),
        scratch_shapes=[
            pltpu.VMEM((1, 512, 512), BF16),
            pltpu.VMEM((1, 512, 512), BF16),
            pltpu.VMEM((EXPERTS_HERE, 128, 2 * FFE), BF16),
            pltpu.VMEM((EXPERTS_HERE, FFE, 128), BF16),
            pltpu.VMEM((8, 128, HEAD), BF16),
            pltpu.VMEM((8, 128, HEAD), BF16),
            pltpu.VMEM((HEAD, 1024), BF16),
            pltpu.VMEM((1024, 128), F32),
            pltpu.VMEM((128, 128), F32),
            pltpu.VMEM((N, 8, HEAD), BF16),
            pltpu.VMEM((N, 128, HEAD), BF16),
            pltpu.VMEM((N, 144, 128), BF16),
            pltpu.VMEM((N, 144, 128), BF16),
            pltpu.VMEM((4, 32, 256), BF16),
            pltpu.VMEM((4, 32, 256), BF16),
            pltpu.VMEM((N, 8, 128), F32),
            pltpu.VMEM((N, 8, 128), F32),
            pltpu.VMEM((N, 32, 128), BF16),
            pltpu.VMEM((N, 16, 128), BF16),
            pltpu.VMEM((N, 16, 128), BF16),
            pltpu.VMEM((N, 16, 128), BF16),
            pltpu.VMEM((TOKENS, TOKENS), BF16),
            pltpu.VMEM((TOKENS, TOKENS), BF16),
            pltpu.VMEM((TOKENS, 128), F32),
            pltpu.VMEM((TOKENS, 256), BF16),
            pltpu.VMEM((N, 16, WIDE), BF16),
            pltpu.VMEM((N, 16, WIDE), BF16),
            pltpu.VMEM((N, 16, FFE), BF16),
            pltpu.VMEM((TOKENS, 256), BF16),
            pltpu.VMEM((N, 16, 128), BF16),
            pltpu.VMEM((N, 16, 128), BF16),
            dma(6),
            dma(8), dma(8),
            dma(N), dma(N),
            dma(N), dma(N),
            dma(N), dma(N),
            dma(4), dma(4),
            dma(N), dma(N),
            dma(N), dma(N),
            dma(N), dma(N),
            dma(N), dma(N),
            dma(N), dma(N),
            dma(N), dma(N),
            dma(N), dma(N),
        ],
        compiler_params=pltpu.CompilerParams(
            collective_id=0, has_side_effects=True, vmem_limit_bytes=48 << 20
        ),
    )(
        fresh_queries.reshape(4, 8, HEAD),
        fresh_key.reshape(4, HEAD),
        fresh_value.reshape(4, HEAD),
        request_own_keys,
        request_own_values,
        leaf_len,
        prefix_pool_keys,
        prefix_pool_values,
        page_table.reshape(1, 512),
        root_len,
        mid_len,
        mid_parent,
        leaf_parent.reshape(1, TOKENS),
        residual,
        out_weight,
        post_gain.reshape(1, 128),
        expert_ids.T,
        gate_weight.T,
        w_gate_up,
        w_down,
    )


def solution(mesh):
    placed = (
        P(("row", "col"), None),
        P(("row", "col"), None),
        P(("row", "col"), None),
        P(("row", "col"), None, None),
        P(("row", "col"), None, None),
        P(("row", "col")),
        P(("row", "col"), None, None),
        P(("row", "col"), None, None),
        P(),
        P(),
        P(),
        P(),
        P(),
        P(None, "row"),
        P("col", "row"),
        P("row"),
        P(),
        P(),
        P("col", "row", None),
        P("col", None, "row"),
    )
    return jax.shard_map(
        per_device,
        mesh=mesh,
        in_specs=placed,
        out_specs=(P(None, "row"), P("col", "row")),
        check_vma=False,
    )
```

```python
import functools
import math

import jax
import jax.numpy as jnp
from jax import lax
from jax.experimental import pallas as pl
from jax.experimental.pallas import tpu as pltpu
from jax.sharding import PartitionSpec as P

D = 2048
HEAD = 128
FFE = 768
ROOTS = 4
MIDS = 32
ROOT_PAGES = 32
MID_PAGES = 12
N = 16
TOKENS = 256
CAP = 32
EXPERTS_HERE = 8
WIDE = 2 * FFE + 128
EPS = 1e-06
DEAD = -float(2**99)
LOG2E = math.log2(math.e)
SCORE = LOG2E / math.sqrt(HEAD)
MESH = pl.DeviceIdType.MESH
F32 = jnp.float32
BF16 = jnp.bfloat16


def dot(a, b):
    return jnp.dot(a, b, preferred_element_type=F32)


def dot_nt(a, b):
    return lax.dot_general(a, b, (((1,), (1,)), ((), ())), preferred_element_type=F32)


def iota(shape, axis):
    return lax.broadcasted_iota(jnp.int32, shape, axis)


def kernel(
    q_hbm,
    fk_hbm,
    fv_hbm,
    ownk_hbm,
    ownv_hbm,
    leaf_len_hbm,
    pk_hbm,
    pv_hbm,
    pt_hbm,
    root_len_hbm,
    mid_len_hbm,
    mid_parent_hbm,
    lp_hbm,
    resid_hbm,
    ow_hbm,
    gain_hbm,
    ids_hbm,
    gw_hbm,
    wgu_hbm,
    wdn_hbm,
    att_ref,
    lay_ref,
    q_in,
    fk_ref,
    fv_ref,
    pt_ref,
    lp_ref,
    resid_ref,
    ow_ref,
    gain_ref,
    ids_ref,
    gw_ref,
    leaf_len,
    root_len,
    mid_len,
    mid_parent,
    q_rows,
    q_ref,
    ownk,
    ownv,
    wgu,
    wdn,
    kst,
    vst,
    kraw,
    kfeat,
    vbuf,
    vt,
    feat,
    qfeat,
    q1buf,
    qblk,
    sacc,
    racc,
    msg,
    rmsg,
    lsend,
    lrecv,
    attnb,
    psend,
    precv,
    attb,
    disp,
    dispt,
    slotw,
    rin,
    gsend,
    grecv,
    actb,
    yb,
    msend,
    mrecv,
    loc_sem,
    kv_s,
    kv_r,
    q1_s,
    q1_r,
    q2_s,
    q2_r,
    ac_s,
    ac_r,
    ms_s,
    ms_r,
    lf_s,
    lf_r,
    an_s,
    an_r,
    pr_s,
    pr_r,
    at_s,
    at_r,
    gu_s,
    gu_r,
    av_s,
    av_r,
    mx_s,
    mx_r,
):
    r = lax.axis_index("row")
    c = lax.axis_index("col")
    z = c // 2
    core = lax.rem(c, 2)
    kv = lax.rem(z, 4)

    def remote(src, dst, ssem, rsem, dev):
        return pltpu.make_async_remote_copy(
            src_ref=src, dst_ref=dst, send_sem=ssem, recv_sem=rsem, device_id=dev, device_id_type=MESH
        )

    def all_here(buf, sem):
        block = buf.at[pl.ds(0, N - 1)]
        pltpu.make_async_copy(block, block, sem).wait()

    def row_mate(i):
        return lax.rem(c + i, N)

    def col_mate(i):
        return lax.rem(r + i, N)

    stage = [
        pltpu.make_async_copy(
            src.at[:, :, k * HEAD : (k + 1) * HEAD], dst.at[k], loc_sem.at[20 + which * 4 + k]
        )
        for which, (src, dst) in enumerate(((pk_hbm, kst), (pv_hbm, vst)))
        for k in range(4)
    ]
    leaf_k = pltpu.make_async_copy(ownk_hbm, ownk, loc_sem.at[2])
    leaf_v = pltpu.make_async_copy(ownv_hbm, ownv, loc_sem.at[3])
    load_gu = pltpu.make_async_copy(wgu_hbm, wgu, loc_sem.at[4])
    load_dn = pltpu.make_async_copy(wdn_hbm, wdn, loc_sem.at[5])
    load_q = pltpu.make_async_copy(q_hbm, q_in, loc_sem.at[6])
    load_q.start()
    early = [
        pltpu.make_async_copy(src, dst, loc_sem.at[7 + i])
        for i, (src, dst) in enumerate(
            (
                (pt_hbm, pt_ref),
                (lp_hbm, lp_ref),
                (root_len_hbm, root_len),
                (mid_len_hbm, mid_len),
                (mid_parent_hbm, mid_parent),
            )
        )
    ]
    second = [
        pltpu.make_async_copy(src, dst, loc_sem.at[12 + i])
        for i, (src, dst) in enumerate(((fk_hbm, fk_ref), (fv_hbm, fv_ref), (leaf_len_hbm, leaf_len)))
    ]
    late = [
        pltpu.make_async_copy(src, dst, loc_sem.at[15 + i])
        for i, (src, dst) in enumerate(
            (
                (ids_hbm, ids_ref),
                (gw_hbm, gw_ref),
                (resid_hbm.at[pl.ds(pl.multiple_of(c * 16, 16), 16)], resid_ref),
                (ow_hbm, ow_ref),
                (gain_hbm, gain_ref),
            )
        )
    ]
    for cp in stage:
        cp.start()
    for cp in early + second:
        cp.start()
    leaf_k.start()
    leaf_v.start()
    for cp in late:
        cp.start()
    load_gu.start()
    load_dn.start()

    barrier = pltpu.get_barrier_semaphore()

    def greet(i, carry):
        pl.semaphore_signal(barrier, inc=1, device_id=(r, row_mate(i)), device_id_type=MESH)
        pl.semaphore_signal(barrier, inc=1, device_id=(col_mate(i), c), device_id_type=MESH)
        return carry

    lax.fori_loop(1, N, greet, 0)
    load_q.wait()
    row = q_in[...].astype(F32)
    for h in range(32):
        q_rows[h : h + 1, :] = row[:, h * HEAD : (h + 1) * HEAD]
    q_ref[...] = q_rows[...].astype(BF16).reshape(4, 8, HEAD)
    for cp in early:
        cp.wait()

    lp = lp_ref[...]
    root_of = jnp.zeros((1, TOKENS), jnp.int32)
    for m in range(MIDS):
        root_of = jnp.where(lp == m, mid_parent[m], root_of)
    slot8 = iota((8, 1), 0)
    far = jnp.where(slot8 == 6, 6, 2)
    from_z = lax.rem(
        z + jnp.where(slot8 < 2, 0, jnp.where(slot8 < 4, 7, jnp.where(slot8 < 6, 1, far))), 8
    )
    page_of = jnp.where(slot8 < 6, jnp.bitwise_and(slot8, 1), slot8 - 6)
    page_id = 2 * (r * N + 2 * from_z + core) + page_of
    place = jnp.sum(
        jnp.where(pt_ref[...] == page_id, iota((8, 512), 1), 0).astype(F32), axis=1, keepdims=True
    ).astype(jnp.int32)
    owner = jnp.zeros((8, 1), jnp.int32)
    first = jnp.zeros((8, 1), jnp.int32)
    length = jnp.zeros((8, 1), jnp.int32)
    root_slots = ROOTS * ROOT_PAGES
    for m in range(ROOTS):
        hit = (place >= m * ROOT_PAGES) & (place < (m + 1) * ROOT_PAGES)
        owner = jnp.where(hit, m, owner)
        first = jnp.where(hit, m * ROOT_PAGES, first)
        length = jnp.where(hit, root_len[m], length)
    for m in range(MIDS):
        lo = root_slots + m * MID_PAGES
        hit = (place >= lo) & (place < lo + MID_PAGES)
        owner = jnp.where(hit, m, owner)
        first = jnp.where(hit, lo, first)
        length = jnp.where(hit, mid_len[m], length)
    alive = length - (place - first) * HEAD
    owned = jnp.where(place < root_slots, root_of, lp) == owner
    missing = jnp.concatenate(
        [jnp.where(owned, 0.0, 1.0), jnp.ones((1, TOKENS), F32), jnp.zeros((119, TOKENS), F32)], axis=0
    )
    feat[...] = (missing.T * DEAD).astype(BF16)
    lane = iota((128, 128), 1)
    for p in range(8):
        limit = jnp.broadcast_to(alive[p : p + 1, :], (128, 128))
        dead = jnp.where(iota((128, 128), 0) < limit, 0.0, 1.0)
        kfeat[p] = jnp.where(lane == p, 1.0, jnp.where(lane == 8, dead, 0.0)).astype(BF16)

    def spread(b, carry):
        some = feat[pl.ds(pl.multiple_of(b * 16, 16), 16), :]
        for g in range(8):
            qfeat[b, g * 16 : (g + 1) * 16, :] = some
        return carry

    lax.fori_loop(0, N, spread, 0)

    for cp in second:
        cp.wait()
    leaf_k.wait()
    leaf_v.wait()
    for k in range(4):
        q8 = q_ref[k]
        s = dot_nt(q8, ownk[0, :, k * HEAD : (k + 1) * HEAD])
        s = jnp.where(iota((8, 512), 1) < leaf_len[0], s, DEAD)
        fresh = jnp.sum(q8.astype(F32) * fk_ref[:, k * HEAD : (k + 1) * HEAD].astype(F32), axis=1, keepdims=True)
        m = jnp.maximum(jnp.max(s, axis=1, keepdims=True), fresh)
        p = jnp.exp2((s - m) * SCORE)
        pf = jnp.exp2((fresh - m) * SCORE)
        total = jnp.sum(p, axis=1, keepdims=True) + pf
        acc = dot(p.astype(BF16), ownv[0, :, k * HEAD : (k + 1) * HEAD]) + pf * fv_ref[:, k * HEAD : (k + 1) * HEAD].astype(F32)
        m = jnp.broadcast_to(m, (8, HEAD))
        total = jnp.broadcast_to(total, (8, HEAD))
        for j in range(4):
            two = slice(2 * j, 2 * j + 2)
            lsend[4 * k + j] = jnp.concatenate([acc[two], m[two], total[two], total[two]], axis=0)

    for cp in stage:
        cp.wait()
    pl.semaphore_wait(barrier, 2 * (N - 1))

    def q1_copy(i):
        to = row_mate(i)
        head = lax.rem(to // 2, 4)
        return remote(q_ref.at[head], q1buf.at[c], q1_s.at[0], q1_r.at[0], (r, to))

    def q1_start(i, carry):
        q1_copy(i).start()
        return carry

    lax.fori_loop(1, N, q1_start, 0)

    def kv_copies():
        out = []
        for which, (src, dst) in enumerate(((kst, kraw), (vst, vbuf))):
            for step, first, pages, slot in ((1, 0, 2, 2), (7, 0, 2, 4), (2, 0, 1, 6), (6, 1, 1, 7)):
                zt = lax.rem(z + step, 8)
                out.append(
                    remote(
                        src.at[lax.rem(zt, 4), pl.ds(first, pages)],
                        dst.at[pl.ds(slot, pages)],
                        kv_s.at[which],
                        kv_r.at[which],
                        (r, zt * 2 + core),
                    )
                )
        return out

    kv_list = kv_copies()
    for cp in kv_list:
        cp.start()
    q1buf[c] = q_ref[kv]

    all_here(q1buf, q1_r.at[0])
    order = jnp.where(
        iota((128, 128), 1) == lax.rem(iota((128, 128), 0), N) * 8 + iota((128, 128), 0) // N, 1.0, 0.0
    ).astype(BF16)
    qblk[r] = dot(order, q1buf[...].reshape(128, HEAD)).astype(BF16)

    def q2_copy(i):
        to = col_mate(i)
        return remote(qblk.at[r], qblk.at[r], q2_s.at[0], q2_r.at[r], (to, c))

    def q2_start(i, carry):
        q2_copy(i).start()
        return carry

    lax.fori_loop(1, N, q2_start, 0)

    def leaf_copy(i):
        to = row_mate(i)
        return remote(lsend.at[to], lrecv.at[c], lf_s.at[0], lf_r.at[0], (r, to))

    def leaf_start(i, carry):
        leaf_copy(i).start()
        return carry

    lax.fori_loop(1, N, leaf_start, 0)
    lrecv[c] = lsend[c]

    kraw[0:2] = kst[kv]
    vbuf[0:2] = vst[kv]
    for p in range(2):
        vt[:, p * 128 : (p + 1) * 128] = vbuf[p].astype(F32).T.astype(BF16)
    for which, buf in enumerate((kraw, vbuf)):
        six = buf.at[pl.ds(2, 6)]
        pltpu.make_async_copy(six, six, kv_r.at[which]).wait()
    for p in range(2, 8):
        vt[:, p * 128 : (p + 1) * 128] = vbuf[p].astype(F32).T.astype(BF16)

    def acc_copy(b):
        return remote(sacc.at[b], racc.at[r], ac_s.at[0], ac_r.at[0], (b, c))

    def attend(i, carry):
        blocks = (col_mate(2 * i), col_mate(2 * i + 1))
        for b in blocks:

            @pl.when(b != r)
            def _():
                remote(qblk.at[r], qblk.at[b], q2_s.at[0], q2_r.at[b], (b, c)).wait_recv()

        keys = jnp.concatenate([kraw[...].reshape(1024, HEAD), kfeat[...].reshape(1024, 128)], axis=1)
        q = jnp.concatenate([jnp.concatenate([qblk[b], qfeat[b]], axis=1) for b in blocks], axis=0)
        s = dot_nt(keys, q)
        m = jnp.max(s, axis=0, keepdims=True).astype(BF16).astype(F32)
        p = jnp.exp2((s - m) * SCORE)
        total = jnp.sum(p, axis=0, keepdims=True)
        acc = dot(vt[...], p.astype(BF16)).astype(BF16)
        hi = total.astype(BF16).astype(F32)
        row = iota((16, 256), 0)
        tail = jnp.where(row == 0, m, jnp.where(row == 1, hi, jnp.where(row == 2, total - hi, 0.0)))
        tail = tail.astype(BF16)
        for n, b in enumerate(blocks):
            sacc[b, 0:128, :] = acc[:, n * 128 : (n + 1) * 128]
            sacc[b, 128:144, :] = tail[:, n * 128 : (n + 1) * 128]

            @pl.when(b != r)
            def _():
                acc_copy(b).start()

        return carry

    lax.fori_loop(0, N // 2, attend, 0)

    for cp in late:
        cp.wait()
    ids = ids_ref[...]
    gw = gw_ref[...]
    chosen, weight = [], []
    for e in range(EXPERTS_HERE):
        hit = ids == c * EXPERTS_HERE + e
        chosen.append(jnp.max(jnp.where(hit, 1.0, 0.0), axis=0, keepdims=True))
        weight.append(jnp.sum(jnp.where(hit, gw, 0.0), axis=0, keepdims=True))
    picks = jnp.concatenate(chosen, axis=0)
    upto = jnp.where(iota((TOKENS, TOKENS), 0) <= iota((TOKENS, TOKENS), 1), 1.0, 0.0).astype(BF16)
    rank = dot(picks.astype(BF16), upto) - 1.0
    for e in range(EXPERTS_HERE):
        slot = iota((CAP, TOKENS), 0).astype(F32)
        one = jnp.where((rank[e : e + 1, :] == slot) & (picks[e : e + 1, :] > 0.5), 1.0, 0.0)
        disp[e * CAP : (e + 1) * CAP, :] = one.astype(BF16)
        slotw[e * CAP : (e + 1) * CAP, :] = jnp.broadcast_to(
            jnp.sum(one * weight[e], axis=1, keepdims=True), (CAP, 128)
        )
    dispt[...] = disp[...].astype(F32).T.astype(BF16)

    racc[r] = sacc[r]

    all_here(racc, ac_r.at[0])
    top = jnp.max(racc[:, 128:144, :].astype(F32)[:, 0:1, :], axis=0)

    def acc_add(i, carry):
        acc, total = carry
        tail = racc[i, 128:144, :].astype(F32)
        f = jnp.exp2((tail[0:1, :] - top) * SCORE)
        return acc + racc[i, 0:128, :].astype(F32) * f, total + (tail[1:2, :] + tail[2:3, :]) * f

    acc, total = lax.fori_loop(0, N, acc_add, (jnp.zeros((128, 128), F32), jnp.zeros((1, 128), F32)))
    hi = total.astype(BF16).astype(F32)
    row = iota((128, 128), 0)
    tail = jnp.where(row == 0, top, jnp.where(row == 1, hi, jnp.where(row == 2, total - hi, 0.0)))
    msg[:, :, 0:128] = acc.T.astype(BF16).reshape(4, 32, 128)
    msg[:, :, 128:256] = tail.T.astype(BF16).reshape(4, 32, 128)
    here = z // 4 * 2 + core

    for j in range(4):
        to = 4 * kv + j

        @pl.when(to != c)
        def _():
            remote(msg.at[j], rmsg.at[here], ms_s.at[j], ms_r.at[0], (r, to)).start()

        @pl.when(to == c)
        def _():
            pltpu.make_async_copy(msg.at[j], rmsg.at[here], ms_r.at[0]).start()

    all_here(lrecv, lf_r.at[0])
    leaf_acc = jnp.concatenate([lrecv[:, 0, :], lrecv[:, 1, :]], axis=0)
    leaf_m = jnp.concatenate([lrecv[:, 2, :], lrecv[:, 3, :]], axis=0)
    leaf_t = jnp.concatenate([lrecv[:, 4, :], lrecv[:, 5, :]], axis=0)
    pltpu.make_async_copy(msg, rmsg, ms_r.at[0]).wait()
    parts = []
    top = leaf_m
    for s in range(4):
        tail = rmsg[s, :, 128:256].astype(F32)
        m = jnp.broadcast_to(tail[:, 0:1], (32, 128))
        parts.append((m, tail[:, 1:2] + tail[:, 2:3], rmsg[s, :, 0:128].astype(F32)))
        top = jnp.maximum(top, m)
    f = jnp.exp2((leaf_m - top) * SCORE)
    acc, total = leaf_acc * f, leaf_t * f
    for m, t, a in parts:
        f = jnp.exp2((m - top) * SCORE)
        acc = acc + a * f
        total = total + t * f
    attnb[r] = (acc / total).astype(BF16)

    def an_copy(i):
        return remote(attnb.at[r], attnb.at[r], an_s.at[0], an_r.at[0], (col_mate(i), c))

    def an_start(i, carry):
        an_copy(i).start()
        return carry

    lax.fori_loop(1, N, an_start, 0)
    all_here(attnb, an_r.at[0])

    proj = dot(attnb[:, 0:16, :].reshape(TOKENS, HEAD), ow_ref[0:HEAD, :])
    proj = proj + dot(attnb[:, 16:32, :].reshape(TOKENS, HEAD), ow_ref[HEAD : 2 * HEAD, :])
    psend[...] = proj.astype(BF16).reshape(N, 16, 128)

    def pr_copy(i):
        to = row_mate(i)
        return remote(psend.at[to], precv.at[c], pr_s.at[0], pr_r.at[0], (r, to))

    def pr_start(i, carry):
        pr_copy(i).start()
        return carry

    lax.fori_loop(1, N, pr_start, 0)
    precv[c] = psend[c]
    all_here(precv, pr_r.at[0])
    own_att = resid_ref[...].astype(F32) + jnp.sum(precv[...].astype(F32), axis=0)
    attb[c] = own_att.astype(BF16)

    def at_copy(i):
        to = row_mate(i)
        return remote(attb.at[c], attb.at[c], at_s.at[0], at_r.at[0], (r, to))

    def at_start(i, carry):
        at_copy(i).start()
        return carry

    lax.fori_loop(1, N, at_start, 0)

    all_here(attb, at_r.at[0])
    att = attb[...].reshape(TOKENS, 128)
    att_ref[...] = att

    wide = att.astype(F32)
    squares = jnp.sum(wide * wide, axis=1, keepdims=True)
    hi = squares.astype(BF16).astype(F32)
    lane = iota((TOKENS, 128), 1)
    side = jnp.where(lane == 0, hi, jnp.where(lane == 1, squares - hi, 0.0))
    scaled = (wide * gain_ref[...]).astype(BF16)
    rin[...] = dot(disp[...], jnp.concatenate([scaled, side.astype(BF16)], axis=1)).astype(BF16)
    load_gu.wait()

    def gu_copy(to):
        return remote(gsend.at[to], grecv.at[r], gu_s.at[0], gu_r.at[0], (to, c))

    def gate_up(i, carry):
        e = lax.rem(r // 2 + i, EXPERTS_HERE)
        rows = rin[pl.ds(pl.multiple_of(e * CAP, CAP), CAP), :]
        part = dot(rows[:, 0:128], wgu[e]).astype(BF16)
        for half in range(2):
            to = 2 * e + half
            cut = slice(16 * half, 16 * half + 16)
            gsend[to, :, 0 : 2 * FFE] = part[cut, :]
            gsend[to, :, 2 * FFE : WIDE] = rows[cut, 128:256]

            @pl.when(to != r)
            def _():
                gu_copy(to).start()

        return carry

    lax.fori_loop(0, EXPERTS_HERE, gate_up, 0)
    grecv[r] = gsend[r]

    all_here(grecv, gu_r.at[0])

    def gu_add(i, acc):
        return acc + grecv[i].astype(F32)

    gu = lax.fori_loop(0, N, gu_add, jnp.zeros((16, WIDE), F32))
    inverse = lax.rsqrt((gu[:, 2 * FFE : 2 * FFE + 1] + gu[:, 2 * FFE + 1 : 2 * FFE + 2]) / D + EPS)
    gate = gu[:, 0:FFE] * inverse
    up = gu[:, FFE : 2 * FFE] * inverse
    actb[r] = (gate / (1.0 + jnp.exp(-gate)) * up).astype(BF16)

    def av_copy(i):
        to = col_mate(i)
        return remote(actb.at[r], actb.at[r], av_s.at[0], av_r.at[0], (to, c))

    def av_start(i, carry):
        av_copy(i).start()
        return carry

    lax.fori_loop(1, N, av_start, 0)
    load_dn.wait()

    all_here(actb, av_r.at[0])

    def down(e, carry):
        rows = actb[pl.ds(2 * e, 2)].reshape(CAP, FFE)
        at = pl.ds(pl.multiple_of(e * CAP, CAP), CAP)
        y = dot(rows, wdn[e]) * slotw[at, :]
        hi = y.astype(BF16)
        yb[at, 0:128] = hi
        yb[at, 128:256] = (y - hi.astype(F32)).astype(BF16)
        return carry

    lax.fori_loop(0, EXPERTS_HERE, down, 0)
    mixed = dot(dispt[...], yb[...])
    msend[...] = (mixed[:, 0:128] + mixed[:, 128:256]).astype(BF16).reshape(N, 16, 128)

    def mx_copy(i):
        to = row_mate(i)
        return remote(msend.at[to], mrecv.at[c], mx_s.at[0], mx_r.at[0], (r, to))

    def mx_start(i, carry):
        mx_copy(i).start()
        return carry

    lax.fori_loop(1, N, mx_start, 0)
    mrecv[c] = msend[c]

    all_here(mrecv, mx_r.at[0])
    lay_ref[...] = (attb[c].astype(F32) + jnp.sum(mrecv[...].astype(F32), axis=0)).astype(BF16)

    for which, buf in enumerate((kraw, vbuf)):
        six = buf.at[pl.ds(2, 6)]
        pltpu.make_async_copy(six, six, kv_s.at[which]).wait()
    all_here(q1buf, q1_s.at[0])
    all_here(qblk, q2_s.at[0])
    all_here(lsend, lf_s.at[0])
    all_here(sacc, ac_s.at[0])
    all_here(attnb, an_s.at[0])
    all_here(psend, pr_s.at[0])
    all_here(attb, at_s.at[0])
    all_here(gsend, gu_s.at[0])
    all_here(actb, av_s.at[0])
    all_here(msend, mx_s.at[0])
    for j in range(4):
        to = 4 * kv + j

        @pl.when(to != c)
        def _():
            remote(msg.at[j], rmsg.at[here], ms_s.at[j], ms_r.at[0], (r, to)).wait_send()


def per_device(
    fresh_queries,
    fresh_key,
    fresh_value,
    request_own_keys,
    request_own_values,
    leaf_len,
    prefix_pool_keys,
    prefix_pool_values,
    page_table,
    root_len,
    mid_len,
    mid_parent,
    leaf_parent,
    residual,
    out_weight,
    post_gain,
    expert_ids,
    gate_weight,
    w_gate_up,
    w_down,
):
    vmem = pl.BlockSpec(memory_space=pltpu.VMEM)
    hbm = pl.BlockSpec(memory_space=pltpu.HBM)
    dma = lambda n: pltpu.SemaphoreType.DMA((n,))
    return pl.pallas_call(
        kernel,
        out_shape=(
            jax.ShapeDtypeStruct((TOKENS, 128), BF16),
            jax.ShapeDtypeStruct((16, 128), BF16),
        ),
        in_specs=[hbm] * 20,
        out_specs=(vmem, vmem),
        scratch_shapes=[
            pltpu.VMEM((1, 4096), BF16),
            pltpu.VMEM((1, 512), BF16),
            pltpu.VMEM((1, 512), BF16),
            pltpu.VMEM((1, 512), jnp.int32),
            pltpu.VMEM((1, TOKENS), jnp.int32),
            pltpu.VMEM((16, 128), BF16),
            pltpu.VMEM((TOKENS, 128), BF16),
            pltpu.VMEM((1, 128), F32),
            pltpu.VMEM((8, TOKENS), jnp.int32),
            pltpu.VMEM((8, TOKENS), F32),
            pltpu.SMEM((1,), jnp.int32),
            pltpu.SMEM((ROOTS,), jnp.int32),
            pltpu.SMEM((MIDS,), jnp.int32),
            pltpu.SMEM((MIDS,), jnp.int32),
            pltpu.VMEM((32, HEAD), F32),
            pltpu.VMEM((4, 8, HEAD), BF16),
            pltpu.VMEM((1, 512, 512), BF16),
            pltpu.VMEM((1, 512, 512), BF16),
            pltpu.VMEM((EXPERTS_HERE, 128, 2 * FFE), BF16),
            pltpu.VMEM((EXPERTS_HERE, FFE, 128), BF16),
            pltpu.VMEM((4, 2, 128, HEAD), BF16),
            pltpu.VMEM((4, 2, 128, HEAD), BF16),
            pltpu.VMEM((8, 128, HEAD), BF16),
            pltpu.VMEM((8, 128, 128), BF16),
            pltpu.VMEM((8, 128, HEAD), BF16),
            pltpu.VMEM((HEAD, 1024), BF16),
            pltpu.VMEM((TOKENS, 128), BF16),
            pltpu.VMEM((N, 128, 128), BF16),
            pltpu.VMEM((N, 8, HEAD), BF16),
            pltpu.VMEM((N, 128, HEAD), BF16),
            pltpu.VMEM((N, 144, 128), BF16),
            pltpu.VMEM((N, 144, 128), BF16),
            pltpu.VMEM((4, 32, 256), BF16),
            pltpu.VMEM((4, 32, 256), BF16),
            pltpu.VMEM((N, 8, 128), F32),
            pltpu.VMEM((N, 8, 128), F32),
            pltpu.VMEM((N, 32, 128), BF16),
            pltpu.VMEM((N, 16, 128), BF16),
            pltpu.VMEM((N, 16, 128), BF16),
            pltpu.VMEM((N, 16, 128), BF16),
            pltpu.VMEM((TOKENS, TOKENS), BF16),
            pltpu.VMEM((TOKENS, TOKENS), BF16),
            pltpu.VMEM((TOKENS, 128), F32),
            pltpu.VMEM((TOKENS, 256), BF16),
            pltpu.VMEM((N, 16, WIDE), BF16),
            pltpu.VMEM((N, 16, WIDE), BF16),
            pltpu.VMEM((N, 16, FFE), BF16),
            pltpu.VMEM((TOKENS, 256), BF16),
            pltpu.VMEM((N, 16, 128), BF16),
            pltpu.VMEM((N, 16, 128), BF16),
            dma(28),
            dma(2), dma(2),
            dma(1), dma(1),
            dma(1), dma(N),
            dma(1), dma(1),
            dma(4), dma(1),
            dma(1), dma(1),
            dma(1), dma(1),
            dma(1), dma(1),
            dma(1), dma(1),
            dma(1), dma(1),
            dma(1), dma(1),
            dma(1), dma(1),
        ],
        compiler_params=pltpu.CompilerParams(
            collective_id=0, has_side_effects=True
        ),
    )(
        fresh_queries,
        fresh_key,
        fresh_value,
        request_own_keys,
        request_own_values,
        leaf_len,
        prefix_pool_keys,
        prefix_pool_values,
        page_table.reshape(1, 512),
        root_len,
        mid_len,
        mid_parent,
        leaf_parent.reshape(1, TOKENS),
        residual,
        out_weight,
        post_gain.reshape(1, 128),
        expert_ids.T,
        gate_weight.T,
        w_gate_up,
        w_down,
    )


def solution(mesh):
    placed = (
        P(("row", "col"), None),
        P(("row", "col"), None),
        P(("row", "col"), None),
        P(("row", "col"), None, None),
        P(("row", "col"), None, None),
        P(("row", "col")),
        P(("row", "col"), None, None),
        P(("row", "col"), None, None),
        P(),
        P(),
        P(),
        P(),
        P(),
        P(None, "row"),
        P("col", "row"),
        P("row"),
        P(),
        P(),
        P("col", "row", None),
        P("col", None, "row"),
    )
    return jax.shard_map(
        per_device,
        mesh=mesh,
        in_specs=placed,
        out_specs=(P(None, "row"), P("col", "row")),
        check_vma=False,
    )
```

```python
import functools
import math

import jax
import jax.numpy as jnp
from jax import lax
from jax.experimental import pallas as pl
from jax.experimental.pallas import tpu as pltpu
from jax.sharding import PartitionSpec as P

D = 2048
HEAD = 128
FFE = 768
ROOTS = 4
MIDS = 32
ROOT_PAGES = 32
MID_PAGES = 12
N = 16
TOKENS = 256
CAP = 32
EXPERTS_HERE = 8
WIDE = 2 * FFE + 128
EPS = 1e-06
DEAD = -float(2**99)
LOG2E = math.log2(math.e)
SCORE = LOG2E / math.sqrt(HEAD)
MESH = pl.DeviceIdType.MESH
F32 = jnp.float32
BF16 = jnp.bfloat16


def dot(a, b):
    return jnp.dot(a, b, preferred_element_type=F32)


def dot_nt(a, b):
    return lax.dot_general(a, b, (((1,), (1,)), ((), ())), preferred_element_type=F32)


def iota(shape, axis):
    return lax.broadcasted_iota(jnp.int32, shape, axis)


def kernel(
    q_hbm,
    fk_hbm,
    fv_hbm,
    ownk_hbm,
    ownv_hbm,
    leaf_len_hbm,
    pk_hbm,
    pv_hbm,
    pt_hbm,
    root_len_hbm,
    mid_len_hbm,
    mid_parent_hbm,
    lp_hbm,
    resid_hbm,
    ow_hbm,
    gain_hbm,
    ids_hbm,
    gw_hbm,
    wgu_hbm,
    wdn_hbm,
    att_ref,
    lay_ref,
    q_in,
    fk_ref,
    fv_ref,
    pt_ref,
    lp_ref,
    resid_ref,
    ow_ref,
    gain_ref,
    ids_ref,
    gw_ref,
    leaf_len,
    root_len,
    mid_len,
    mid_parent,
    q_rows,
    q_ref,
    ownk,
    ownv,
    wgu,
    wdn,
    kst,
    vst,
    kraw,
    kfeat,
    vbuf,
    vt,
    feat,
    qfeat,
    q1buf,
    qblk,
    sacc,
    racc,
    turned,
    msg,
    rmsg,
    lsend,
    lrecv,
    attnb,
    psend,
    precv,
    attb,
    disp,
    dispt,
    slotw,
    rin,
    gsend,
    grecv,
    actb,
    yb,
    msend,
    mrecv,
    loc_sem,
    kv_s,
    kv_r,
    fw_s,
    fw_r,
    q1_s,
    q1_r,
    q2_s,
    q2_r,
    ac_s,
    ac_r,
    ms_s,
    ms_r,
    lf_s,
    lf_r,
    an_s,
    an_r,
    pr_s,
    pr_r,
    at_s,
    at_r,
    gu_s,
    gu_r,
    av_s,
    av_r,
    mx_s,
    mx_r,
):
    r = lax.axis_index("row")
    c = lax.axis_index("col")
    z = c // 2
    core = lax.rem(c, 2)
    kv = lax.rem(z, 4)

    def remote(src, dst, ssem, rsem, dev):
        return pltpu.make_async_remote_copy(
            src_ref=src, dst_ref=dst, send_sem=ssem, recv_sem=rsem, device_id=dev, device_id_type=MESH
        )

    def all_here(buf, sem):
        block = buf.at[pl.ds(0, N - 1)]
        pltpu.make_async_copy(block, block, sem).wait()

    def row_mate(i):
        return lax.rem(c + i, N)

    def col_mate(i):
        return lax.rem(r + i, N)

    stage = [
        pltpu.make_async_copy(
            src.at[:, :, k * HEAD : (k + 1) * HEAD], dst.at[k], loc_sem.at[20 + which * 4 + k]
        )
        for which, (src, dst) in enumerate(((pk_hbm, kst), (pv_hbm, vst)))
        for k in range(4)
    ]
    leaf_k = pltpu.make_async_copy(ownk_hbm, ownk, loc_sem.at[2])
    leaf_v = pltpu.make_async_copy(ownv_hbm, ownv, loc_sem.at[3])
    load_gu = pltpu.make_async_copy(wgu_hbm, wgu, loc_sem.at[4])
    load_dn = pltpu.make_async_copy(wdn_hbm, wdn, loc_sem.at[5])
    load_q = pltpu.make_async_copy(q_hbm, q_in, loc_sem.at[6])
    load_q.start()
    early = [
        pltpu.make_async_copy(src, dst, loc_sem.at[7 + i])
        for i, (src, dst) in enumerate(
            (
                (pt_hbm, pt_ref),
                (lp_hbm, lp_ref),
                (root_len_hbm, root_len),
                (mid_len_hbm, mid_len),
                (mid_parent_hbm, mid_parent),
            )
        )
    ]
    second = [
        pltpu.make_async_copy(src, dst, loc_sem.at[12 + i])
        for i, (src, dst) in enumerate(((fk_hbm, fk_ref), (fv_hbm, fv_ref), (leaf_len_hbm, leaf_len)))
    ]
    late = [
        pltpu.make_async_copy(src, dst, loc_sem.at[15 + i])
        for i, (src, dst) in enumerate(
            (
                (ids_hbm, ids_ref),
                (gw_hbm, gw_ref),
                (resid_hbm.at[pl.ds(pl.multiple_of(c * 16, 16), 16)], resid_ref),
                (ow_hbm, ow_ref),
                (gain_hbm, gain_ref),
            )
        )
    ]
    for cp in stage:
        cp.start()
    for cp in early + second:
        cp.start()
    leaf_k.start()
    leaf_v.start()
    for cp in late:
        cp.start()
    load_gu.start()
    load_dn.start()

    barrier = pltpu.get_barrier_semaphore()

    def greet(i, carry):
        pl.semaphore_signal(barrier, inc=1, device_id=(r, row_mate(i)), device_id_type=MESH)
        pl.semaphore_signal(barrier, inc=1, device_id=(col_mate(i), c), device_id_type=MESH)
        return carry

    lax.fori_loop(1, N, greet, 0)
    load_q.wait()
    row = q_in[...].astype(F32)
    for h in range(32):
        q_rows[h : h + 1, :] = row[:, h * HEAD : (h + 1) * HEAD]
    q_ref[...] = q_rows[...].astype(BF16).reshape(4, 8, HEAD)
    for cp in early:
        cp.wait()

    lp = lp_ref[...]
    root_of = jnp.zeros((1, TOKENS), jnp.int32)
    for m in range(MIDS):
        root_of = jnp.where(lp == m, mid_parent[m], root_of)
    slot16 = iota((16, 1), 0)
    slot8 = jnp.bitwise_and(slot16, 7)
    of_core = jnp.where(slot16 < 8, core, 1 - core)
    far = jnp.where(slot8 == 6, 6, 2)
    from_z = lax.rem(
        z + jnp.where(slot8 < 2, 0, jnp.where(slot8 < 4, 7, jnp.where(slot8 < 6, 1, far))), 8
    )
    page_of = jnp.where(slot8 < 6, jnp.bitwise_and(slot8, 1), slot8 - 6)
    page_id = 2 * (r * N + 2 * from_z + of_core) + page_of
    place = jnp.sum(
        jnp.where(pt_ref[...] == page_id, iota((16, 512), 1), 0).astype(F32), axis=1, keepdims=True
    ).astype(jnp.int32)
    owner = jnp.zeros((16, 1), jnp.int32)
    first = jnp.zeros((16, 1), jnp.int32)
    length = jnp.zeros((16, 1), jnp.int32)
    root_slots = ROOTS * ROOT_PAGES
    for m in range(ROOTS):
        hit = (place >= m * ROOT_PAGES) & (place < (m + 1) * ROOT_PAGES)
        owner = jnp.where(hit, m, owner)
        first = jnp.where(hit, m * ROOT_PAGES, first)
        length = jnp.where(hit, root_len[m], length)
    for m in range(MIDS):
        lo = root_slots + m * MID_PAGES
        hit = (place >= lo) & (place < lo + MID_PAGES)
        owner = jnp.where(hit, m, owner)
        first = jnp.where(hit, lo, first)
        length = jnp.where(hit, mid_len[m], length)
    alive = length - (place - first) * HEAD
    owned = jnp.where(place < root_slots, root_of, lp) == owner
    missing = jnp.concatenate(
        [jnp.where(owned, 0.0, 1.0), jnp.ones((1, TOKENS), F32), jnp.zeros((111, TOKENS), F32)], axis=0
    )
    feat[...] = (missing.T * DEAD).astype(BF16)
    lane = iota((128, 128), 1)
    for p in range(16):
        limit = jnp.broadcast_to(alive[p : p + 1, :], (128, 128))
        dead = jnp.where(iota((128, 128), 0) < limit, 0.0, 1.0)
        kfeat[p] = jnp.where(lane == p, 1.0, jnp.where(lane == 16, dead, 0.0)).astype(BF16)

    def spread(b, carry):
        some = feat[pl.ds(pl.multiple_of(b * 16, 16), 16), :]
        for g in range(4):
            qfeat[b, g * 16 : (g + 1) * 16, :] = some
        return carry

    lax.fori_loop(0, N, spread, 0)

    for cp in second:
        cp.wait()
    leaf_k.wait()
    leaf_v.wait()
    for k in range(4):
        q8 = q_ref[k]
        s = dot_nt(q8, ownk[0, :, k * HEAD : (k + 1) * HEAD])
        s = jnp.where(iota((8, 512), 1) < leaf_len[0], s, DEAD)
        fresh = jnp.sum(q8.astype(F32) * fk_ref[:, k * HEAD : (k + 1) * HEAD].astype(F32), axis=1, keepdims=True)
        m = jnp.maximum(jnp.max(s, axis=1, keepdims=True), fresh)
        p = jnp.exp2((s - m) * SCORE)
        pf = jnp.exp2((fresh - m) * SCORE)
        total = jnp.sum(p, axis=1, keepdims=True) + pf
        acc = dot(p.astype(BF16), ownv[0, :, k * HEAD : (k + 1) * HEAD]) + pf * fv_ref[:, k * HEAD : (k + 1) * HEAD].astype(F32)
        m = jnp.broadcast_to(m, (8, HEAD))
        total = jnp.broadcast_to(total, (8, HEAD))
        for j in range(4):
            two = slice(2 * j, 2 * j + 2)
            lsend[4 * k + j] = jnp.concatenate([acc[two], m[two], total[two], total[two]], axis=0)

    for cp in stage:
        cp.wait()
    pl.semaphore_wait(barrier, 2 * (N - 1))

    def q1_copy(i):
        to = row_mate(i)
        head = lax.rem(to // 2, 4)
        return remote(q_ref.at[head], q1buf.at[c], q1_s.at[0], q1_r.at[0], (r, to))

    def q1_start(i, carry):
        q1_copy(i).start()
        return carry

    lax.fori_loop(1, N, q1_start, 0)

    def kv_copies():
        out = []
        for which, (src, dst) in enumerate(((kst, kraw), (vst, vbuf))):
            for step, first, pages, slot in ((1, 0, 2, 2), (7, 0, 2, 4), (2, 0, 1, 6), (6, 1, 1, 7)):
                zt = lax.rem(z + step, 8)
                out.append(
                    remote(
                        src.at[lax.rem(zt, 4), pl.ds(first, pages)],
                        dst.at[pl.ds(slot, pages)],
                        kv_s.at[which],
                        kv_r.at[which],
                        (r, zt * 2 + core),
                    )
                )
        return out

    kv_list = kv_copies()
    for cp in kv_list:
        cp.start()
    sibling = (r, c + 1 - 2 * core)
    own_fw = [
        remote(src.at[kv], dst.at[pl.ds(8, 2)], fw_s.at[which], fw_r.at[which], sibling)
        for which, (src, dst) in enumerate(((kst, kraw), (vst, vbuf)))
    ]
    for cp in own_fw:
        cp.start()
    q1buf[c] = q_ref[kv]

    all_here(q1buf, q1_r.at[0])
    order = jnp.where(
        iota((64, 128), 1) == lax.rem(iota((64, 128), 0), N) * 8 + 4 * core + iota((64, 128), 0) // N, 1.0, 0.0
    ).astype(BF16)
    qblk[r] = dot(order, q1buf[...].reshape(128, HEAD)).astype(BF16)

    def q2_copy(i):
        to = col_mate(i)
        return remote(qblk.at[r], qblk.at[r], q2_s.at[0], q2_r.at[r], (to, c))

    def q2_start(i, carry):
        q2_copy(i).start()
        return carry

    lax.fori_loop(1, N, q2_start, 0)

    def leaf_copy(i):
        to = row_mate(i)
        return remote(lsend.at[to], lrecv.at[c], lf_s.at[0], lf_r.at[0], (r, to))

    def leaf_start(i, carry):
        leaf_copy(i).start()
        return carry

    lax.fori_loop(1, N, leaf_start, 0)
    lrecv[c] = lsend[c]

    for which, buf in enumerate((kraw, vbuf)):
        six = buf.at[pl.ds(2, 6)]
        pltpu.make_async_copy(six, six, kv_r.at[which]).wait()
        remote(six, buf.at[pl.ds(10, 6)], fw_s.at[which], fw_r.at[which], sibling).start()
    kraw[0:2] = kst[kv]
    vbuf[0:2] = vst[kv]
    for p in range(8):
        vt[:, p * 128 : (p + 1) * 128] = vbuf[p].astype(F32).T.astype(BF16)
    for which, buf in enumerate((kraw, vbuf)):
        eight = buf.at[pl.ds(8, 8)]
        pltpu.make_async_copy(eight, eight, fw_r.at[which]).wait()
    for p in range(8, 16):
        vt[:, p * 128 : (p + 1) * 128] = vbuf[p].astype(F32).T.astype(BF16)

    def acc_copy(b):
        return remote(sacc.at[b], racc.at[r], ac_s.at[0], ac_r.at[0], (b, c))

    def attend(i, carry):
        pair = lax.rem(r // 2 + i, N // 2)
        blocks = (2 * pair, 2 * pair + 1)
        for b in blocks:

            @pl.when(b != r)
            def _():
                remote(qblk.at[r], qblk.at[b], q2_s.at[0], q2_r.at[b], (b, c)).wait_recv()

        keys = jnp.concatenate([kraw[...].reshape(2048, HEAD), kfeat[...].reshape(2048, 128)], axis=1)
        q = jnp.concatenate([jnp.concatenate([qblk[b], qfeat[b]], axis=1) for b in blocks], axis=0)
        s = dot_nt(keys, q)
        m = jnp.max(s, axis=0, keepdims=True).astype(BF16).astype(F32)
        p = jnp.exp2((s - m) * SCORE)
        total = jnp.sum(p, axis=0, keepdims=True)
        acc = dot(vt[...], p.astype(BF16)).T.astype(BF16)
        hi = total.astype(BF16).astype(F32)
        row = iota((16, 128), 0)
        tail = jnp.where(row == 0, m, jnp.where(row == 1, hi, jnp.where(row == 2, total - hi, 0.0)))
        tail = tail.astype(BF16)
        for n, b in enumerate(blocks):
            sacc[b, 0:64, :] = acc[n * 64 : (n + 1) * 64, :]
            sacc[b, 64:80, :] = tail

            @pl.when(b != r)
            def _():
                acc_copy(b).start()

        return carry

    lax.fori_loop(0, N // 2, attend, 0)

    for cp in late:
        cp.wait()
    ids = ids_ref[...]
    gw = gw_ref[...]
    chosen, weight = [], []
    for e in range(EXPERTS_HERE):
        hit = ids == c * EXPERTS_HERE + e
        chosen.append(jnp.max(jnp.where(hit, 1.0, 0.0), axis=0, keepdims=True))
        weight.append(jnp.sum(jnp.where(hit, gw, 0.0), axis=0, keepdims=True))
    picks = jnp.concatenate(chosen, axis=0)
    upto = jnp.where(iota((TOKENS, TOKENS), 0) <= iota((TOKENS, TOKENS), 1), 1.0, 0.0).astype(BF16)
    rank = dot(picks.astype(BF16), upto) - 1.0
    for e in range(EXPERTS_HERE):
        slot = iota((CAP, TOKENS), 0).astype(F32)
        one = jnp.where((rank[e : e + 1, :] == slot) & (picks[e : e + 1, :] > 0.5), 1.0, 0.0)
        disp[e * CAP : (e + 1) * CAP, :] = one.astype(BF16)
        slotw[e * CAP : (e + 1) * CAP, :] = jnp.broadcast_to(
            jnp.sum(one * weight[e], axis=1, keepdims=True), (CAP, 128)
        )
    dispt[...] = disp[...].astype(F32).T.astype(BF16)

    racc[r] = sacc[r]

    all_here(racc, ac_r.at[0])
    tails = racc[:, 64:80, :].astype(F32)
    top = jnp.max(tails[:, 0, :], axis=0, keepdims=True)
    scale = jnp.exp2((tails[:, 0, :] - top) * SCORE)
    total = jnp.sum(scale * (tails[:, 1, :] + tails[:, 2, :]), axis=0, keepdims=True)
    hi = total.astype(BF16).astype(F32)
    turned[...] = jnp.concatenate([scale, top, hi, total - hi, jnp.zeros((109, 128), F32)], axis=0).T
    tail = turned[pl.ds(pl.multiple_of(64 * lax.rem(r, 2), 64), 64), :]
    acc = racc[0, 0:64, :].astype(F32) * tail[:, 0:1]
    for i in range(1, N):
        acc = acc + racc[i, 0:64, :].astype(F32) * tail[:, i : i + 1]
    msg[:, :, 0:128] = acc.astype(BF16).reshape(2, 32, 128)
    msg[:, :, 128:256] = tail.astype(BF16).reshape(2, 32, 128)
    here = z // 4

    for j in range(2):
        to = 4 * kv + 2 * core + j

        @pl.when(to != c)
        def _():
            remote(msg.at[j], rmsg.at[here], ms_s.at[j], ms_r.at[0], (r, to)).start()

        @pl.when(to == c)
        def _():
            pltpu.make_async_copy(msg.at[j], rmsg.at[here], ms_r.at[0]).start()

    all_here(lrecv, lf_r.at[0])
    leaf_acc = jnp.concatenate([lrecv[:, 0, :], lrecv[:, 1, :]], axis=0)
    leaf_m = jnp.concatenate([lrecv[:, 2, :], lrecv[:, 3, :]], axis=0)
    leaf_t = jnp.concatenate([lrecv[:, 4, :], lrecv[:, 5, :]], axis=0)
    pltpu.make_async_copy(msg, rmsg, ms_r.at[0]).wait()
    parts = []
    top = leaf_m
    for s in range(2):
        tail = rmsg[s, :, 128:256].astype(F32)
        m = jnp.broadcast_to(tail[:, 16:17], (32, 128))
        parts.append((m, tail[:, 17:18] + tail[:, 18:19], rmsg[s, :, 0:128].astype(F32)))
        top = jnp.maximum(top, m)
    f = jnp.exp2((leaf_m - top) * SCORE)
    acc, total = leaf_acc * f, leaf_t * f
    for m, t, a in parts:
        f = jnp.exp2((m - top) * SCORE)
        acc = acc + a * f
        total = total + t * f
    attnb[r] = (acc / total).astype(BF16)

    def an_copy(i):
        return remote(attnb.at[r], attnb.at[r], an_s.at[0], an_r.at[0], (col_mate(i), c))

    def an_start(i, carry):
        an_copy(i).start()
        return carry

    lax.fori_loop(1, N, an_start, 0)
    all_here(attnb, an_r.at[0])

    proj = dot(attnb[:, 0:16, :].reshape(TOKENS, HEAD), ow_ref[0:HEAD, :])
    proj = proj + dot(attnb[:, 16:32, :].reshape(TOKENS, HEAD), ow_ref[HEAD : 2 * HEAD, :])
    psend[...] = proj.astype(BF16).reshape(N, 16, 128)

    def pr_copy(i):
        to = row_mate(i)
        return remote(psend.at[to], precv.at[c], pr_s.at[0], pr_r.at[0], (r, to))

    def pr_start(i, carry):
        pr_copy(i).start()
        return carry

    lax.fori_loop(1, N, pr_start, 0)
    precv[c] = psend[c]
    all_here(precv, pr_r.at[0])
    own_att = resid_ref[...].astype(F32) + jnp.sum(precv[...].astype(F32), axis=0)
    attb[c] = own_att.astype(BF16)

    def at_copy(i):
        to = row_mate(i)
        return remote(attb.at[c], attb.at[c], at_s.at[0], at_r.at[0], (r, to))

    def at_start(i, carry):
        at_copy(i).start()
        return carry

    lax.fori_loop(1, N, at_start, 0)

    all_here(attb, at_r.at[0])
    att = attb[...].reshape(TOKENS, 128)
    att_ref[...] = att

    wide = att.astype(F32)
    squares = jnp.sum(wide * wide, axis=1, keepdims=True)
    hi = squares.astype(BF16).astype(F32)
    lane = iota((TOKENS, 128), 1)
    side = jnp.where(lane == 0, hi, jnp.where(lane == 1, squares - hi, 0.0))
    scaled = (wide * gain_ref[...]).astype(BF16)
    rin[...] = dot(disp[...], jnp.concatenate([scaled, side.astype(BF16)], axis=1)).astype(BF16)
    load_gu.wait()

    def gu_copy(to):
        return remote(gsend.at[to], grecv.at[r], gu_s.at[0], gu_r.at[0], (to, c))

    def gate_up(i, carry):
        e = lax.rem(r // 2 + i, EXPERTS_HERE)
        rows = rin[pl.ds(pl.multiple_of(e * CAP, CAP), CAP), :]
        part = dot(rows[:, 0:128], wgu[e]).astype(BF16)
        for half in range(2):
            to = 2 * e + half
            cut = slice(16 * half, 16 * half + 16)
            gsend[to, :, 0 : 2 * FFE] = part[cut, :]
            gsend[to, :, 2 * FFE : WIDE] = rows[cut, 128:256]

            @pl.when(to != r)
            def _():
                gu_copy(to).start()

        return carry

    lax.fori_loop(0, EXPERTS_HERE, gate_up, 0)
    grecv[r] = gsend[r]

    all_here(grecv, gu_r.at[0])

    def gu_add(i, acc):
        return acc + grecv[i].astype(F32)

    gu = lax.fori_loop(0, N, gu_add, jnp.zeros((16, WIDE), F32))
    inverse = lax.rsqrt((gu[:, 2 * FFE : 2 * FFE + 1] + gu[:, 2 * FFE + 1 : 2 * FFE + 2]) / D + EPS)
    gate = gu[:, 0:FFE] * inverse
    up = gu[:, FFE : 2 * FFE] * inverse
    actb[r] = (gate / (1.0 + jnp.exp(-gate)) * up).astype(BF16)

    def av_copy(i):
        to = col_mate(i)
        return remote(actb.at[r], actb.at[r], av_s.at[0], av_r.at[0], (to, c))

    def av_start(i, carry):
        av_copy(i).start()
        return carry

    lax.fori_loop(1, N, av_start, 0)
    load_dn.wait()

    all_here(actb, av_r.at[0])

    def down(e, carry):
        rows = actb[pl.ds(2 * e, 2)].reshape(CAP, FFE)
        at = pl.ds(pl.multiple_of(e * CAP, CAP), CAP)
        y = dot(rows, wdn[e]) * slotw[at, :]
        hi = y.astype(BF16)
        yb[at, 0:128] = hi
        yb[at, 128:256] = (y - hi.astype(F32)).astype(BF16)
        return carry

    lax.fori_loop(0, EXPERTS_HERE, down, 0)
    mixed = dot(dispt[...], yb[...])
    msend[...] = (mixed[:, 0:128] + mixed[:, 128:256]).astype(BF16).reshape(N, 16, 128)

    def mx_copy(i):
        to = row_mate(i)
        return remote(msend.at[to], mrecv.at[c], mx_s.at[0], mx_r.at[0], (r, to))

    def mx_start(i, carry):
        mx_copy(i).start()
        return carry

    lax.fori_loop(1, N, mx_start, 0)
    mrecv[c] = msend[c]

    all_here(mrecv, mx_r.at[0])
    lay_ref[...] = (attb[c].astype(F32) + jnp.sum(mrecv[...].astype(F32), axis=0)).astype(BF16)

    for which, buf in enumerate((kraw, vbuf)):
        six = buf.at[pl.ds(2, 6)]
        pltpu.make_async_copy(six, six, kv_s.at[which]).wait()
    for which, buf in enumerate((kraw, vbuf)):
        eight = buf.at[pl.ds(8, 8)]
        pltpu.make_async_copy(eight, eight, fw_s.at[which]).wait()
    all_here(q1buf, q1_s.at[0])
    all_here(qblk, q2_s.at[0])
    all_here(lsend, lf_s.at[0])
    all_here(sacc, ac_s.at[0])
    all_here(attnb, an_s.at[0])
    all_here(psend, pr_s.at[0])
    all_here(attb, at_s.at[0])
    all_here(gsend, gu_s.at[0])
    all_here(actb, av_s.at[0])
    all_here(msend, mx_s.at[0])
    for j in range(2):
        to = 4 * kv + 2 * core + j

        @pl.when(to != c)
        def _():
            remote(msg.at[j], rmsg.at[here], ms_s.at[j], ms_r.at[0], (r, to)).wait_send()


def per_device(
    fresh_queries,
    fresh_key,
    fresh_value,
    request_own_keys,
    request_own_values,
    leaf_len,
    prefix_pool_keys,
    prefix_pool_values,
    page_table,
    root_len,
    mid_len,
    mid_parent,
    leaf_parent,
    residual,
    out_weight,
    post_gain,
    expert_ids,
    gate_weight,
    w_gate_up,
    w_down,
):
    vmem = pl.BlockSpec(memory_space=pltpu.VMEM)
    hbm = pl.BlockSpec(memory_space=pltpu.HBM)
    dma = lambda n: pltpu.SemaphoreType.DMA((n,))
    return pl.pallas_call(
        kernel,
        out_shape=(
            jax.ShapeDtypeStruct((TOKENS, 128), BF16),
            jax.ShapeDtypeStruct((16, 128), BF16),
        ),
        in_specs=[hbm] * 20,
        out_specs=(vmem, vmem),
        scratch_shapes=[
            pltpu.VMEM((1, 4096), BF16),
            pltpu.VMEM((1, 512), BF16),
            pltpu.VMEM((1, 512), BF16),
            pltpu.VMEM((1, 512), jnp.int32),
            pltpu.VMEM((1, TOKENS), jnp.int32),
            pltpu.VMEM((16, 128), BF16),
            pltpu.VMEM((TOKENS, 128), BF16),
            pltpu.VMEM((1, 128), F32),
            pltpu.VMEM((8, TOKENS), jnp.int32),
            pltpu.VMEM((8, TOKENS), F32),
            pltpu.SMEM((1,), jnp.int32),
            pltpu.SMEM((ROOTS,), jnp.int32),
            pltpu.SMEM((MIDS,), jnp.int32),
            pltpu.SMEM((MIDS,), jnp.int32),
            pltpu.VMEM((32, HEAD), F32),
            pltpu.VMEM((4, 8, HEAD), BF16),
            pltpu.VMEM((1, 512, 512), BF16),
            pltpu.VMEM((1, 512, 512), BF16),
            pltpu.VMEM((EXPERTS_HERE, 128, 2 * FFE), BF16),
            pltpu.VMEM((EXPERTS_HERE, FFE, 128), BF16),
            pltpu.VMEM((4, 2, 128, HEAD), BF16),
            pltpu.VMEM((4, 2, 128, HEAD), BF16),
            pltpu.VMEM((16, 128, HEAD), BF16),
            pltpu.VMEM((16, 128, 128), BF16),
            pltpu.VMEM((16, 128, HEAD), BF16),
            pltpu.VMEM((HEAD, 2048), BF16),
            pltpu.VMEM((TOKENS, 128), BF16),
            pltpu.VMEM((N, 64, 128), BF16),
            pltpu.VMEM((N, 8, HEAD), BF16),
            pltpu.VMEM((N, 64, HEAD), BF16),
            pltpu.VMEM((N, 80, 128), BF16),
            pltpu.VMEM((N, 80, 128), BF16),
            pltpu.VMEM((128, 128), F32),
            pltpu.VMEM((2, 32, 256), BF16),
            pltpu.VMEM((2, 32, 256), BF16),
            pltpu.VMEM((N, 8, 128), F32),
            pltpu.VMEM((N, 8, 128), F32),
            pltpu.VMEM((N, 32, 128), BF16),
            pltpu.VMEM((N, 16, 128), BF16),
            pltpu.VMEM((N, 16, 128), BF16),
            pltpu.VMEM((N, 16, 128), BF16),
            pltpu.VMEM((TOKENS, TOKENS), BF16),
            pltpu.VMEM((TOKENS, TOKENS), BF16),
            pltpu.VMEM((TOKENS, 128), F32),
            pltpu.VMEM((TOKENS, 256), BF16),
            pltpu.VMEM((N, 16, WIDE), BF16),
            pltpu.VMEM((N, 16, WIDE), BF16),
            pltpu.VMEM((N, 16, FFE), BF16),
            pltpu.VMEM((TOKENS, 256), BF16),
            pltpu.VMEM((N, 16, 128), BF16),
            pltpu.VMEM((N, 16, 128), BF16),
            dma(28),
            dma(2), dma(2),
            dma(2), dma(2),
            dma(1), dma(1),
            dma(1), dma(N),
            dma(1), dma(1),
            dma(4), dma(1),
            dma(1), dma(1),
            dma(1), dma(1),
            dma(1), dma(1),
            dma(1), dma(1),
            dma(1), dma(1),
            dma(1), dma(1),
            dma(1), dma(1),
        ],
        compiler_params=pltpu.CompilerParams(
            collective_id=0, has_side_effects=True
        ),
    )(
        fresh_queries,
        fresh_key,
        fresh_value,
        request_own_keys,
        request_own_values,
        leaf_len,
        prefix_pool_keys,
        prefix_pool_values,
        page_table.reshape(1, 512),
        root_len,
        mid_len,
        mid_parent,
        leaf_parent.reshape(1, TOKENS),
        residual,
        out_weight,
        post_gain.reshape(1, 128),
        expert_ids.T,
        gate_weight.T,
        w_gate_up,
        w_down,
    )


def solution(mesh):
    placed = (
        P(("row", "col"), None),
        P(("row", "col"), None),
        P(("row", "col"), None),
        P(("row", "col"), None, None),
        P(("row", "col"), None, None),
        P(("row", "col")),
        P(("row", "col"), None, None),
        P(("row", "col"), None, None),
        P(),
        P(),
        P(),
        P(),
        P(),
        P(None, "row"),
        P("col", "row"),
        P("row"),
        P(),
        P(),
        P("col", "row", None),
        P("col", None, "row"),
    )
    return jax.shard_map(
        per_device,
        mesh=mesh,
        in_specs=placed,
        out_specs=(P(None, "row"), P("col", "row")),
        check_vma=False,
    )
```

```python
import functools
import math

import jax
import jax.numpy as jnp
from jax import lax
from jax.experimental import pallas as pl
from jax.experimental.pallas import tpu as pltpu
from jax.sharding import PartitionSpec as P

D = 2048
HEAD = 128
FFE = 768
ROOTS = 4
MIDS = 32
ROOT_PAGES = 32
MID_PAGES = 12
N = 16
TOKENS = 256
CAP = 32
EXPERTS_HERE = 8
WIDE = 2 * FFE + 128
EPS = 1e-06
DEAD = -float(2**99)
LOG2E = math.log2(math.e)
SCORE = LOG2E / math.sqrt(HEAD)
MESH = pl.DeviceIdType.MESH
F32 = jnp.float32
BF16 = jnp.bfloat16


def dot(a, b):
    return jnp.dot(a, b, preferred_element_type=F32)


def dot_nt(a, b):
    return lax.dot_general(a, b, (((1,), (1,)), ((), ())), preferred_element_type=F32)


def iota(shape, axis):
    return lax.broadcasted_iota(jnp.int32, shape, axis)


def kernel(
    q_hbm,
    fk_hbm,
    fv_hbm,
    ownk_hbm,
    ownv_hbm,
    leaf_len_hbm,
    pk_hbm,
    pv_hbm,
    pt_hbm,
    root_len_hbm,
    mid_len_hbm,
    mid_parent_hbm,
    lp_hbm,
    resid_hbm,
    ow_hbm,
    gain_hbm,
    ids_hbm,
    gw_hbm,
    wgu_hbm,
    wdn_hbm,
    att_ref,
    lay_ref,
    q_in,
    fk_ref,
    fv_ref,
    pt_ref,
    lp_ref,
    resid_ref,
    ow_ref,
    gain_ref,
    ids_ref,
    gw_ref,
    leaf_len,
    root_len,
    mid_len,
    mid_parent,
    q_rows,
    q_ref,
    ownk,
    ownv,
    wgu,
    wdn,
    kst,
    vst,
    kraw,
    kfeat,
    vbuf,
    vt,
    feat,
    qfeat,
    q1buf,
    qblk,
    sacc,
    racc,
    turned,
    msg,
    rmsg,
    lsend,
    lrecv,
    attnb,
    psend,
    precv,
    attb,
    disp,
    dispt,
    slotw,
    rin,
    gsend,
    grecv,
    actb,
    yb,
    msend,
    mrecv,
    loc_sem,
    kv_s,
    kv_r,
    fw_s,
    fw_r,
    q1_s,
    q1_r,
    q2_s,
    q2_r,
    ac_s,
    ac_r,
    ms_s,
    ms_r,
    lf_s,
    lf_r,
    an_s,
    an_r,
    pr_s,
    pr_r,
    at_s,
    at_r,
    gu_s,
    gu_r,
    av_s,
    av_r,
    mx_s,
    mx_r,
):
    r = lax.axis_index("row")
    c = lax.axis_index("col")
    z = c // 2
    core = lax.rem(c, 2)
    kv = lax.rem(z, 4)

    def remote(src, dst, ssem, rsem, dev):
        return pltpu.make_async_remote_copy(
            src_ref=src, dst_ref=dst, send_sem=ssem, recv_sem=rsem, device_id=dev, device_id_type=MESH
        )

    def all_here(buf, sem):
        block = buf.at[pl.ds(0, N - 1)]
        pltpu.make_async_copy(block, block, sem).wait()

    def row_mate(i):
        return lax.rem(c + N // 2 + (1 - 2 * lax.rem(i, 2)) * (i // 2), N)

    def col_mate(i):
        k = i - 1 + i // 11
        return lax.rem(r // 4 + k // 4 + 2, 4) * 4 + lax.rem(lax.rem(r, 4) + lax.rem(k, 4) + 2, 4)

    stage = [
        pltpu.make_async_copy(
            src.at[:, :, k * HEAD : (k + 1) * HEAD], dst.at[k], loc_sem.at[20 + which * 4 + k]
        )
        for which, (src, dst) in enumerate(((pk_hbm, kst), (pv_hbm, vst)))
        for k in range(4)
    ]
    leaf_k = pltpu.make_async_copy(ownk_hbm, ownk, loc_sem.at[2])
    leaf_v = pltpu.make_async_copy(ownv_hbm, ownv, loc_sem.at[3])
    load_gu = pltpu.make_async_copy(wgu_hbm, wgu, loc_sem.at[4])
    load_dn = pltpu.make_async_copy(wdn_hbm, wdn, loc_sem.at[5])
    load_q = pltpu.make_async_copy(q_hbm, q_in, loc_sem.at[6])
    load_q.start()
    early = [
        pltpu.make_async_copy(src, dst, loc_sem.at[7 + i])
        for i, (src, dst) in enumerate(
            (
                (pt_hbm, pt_ref),
                (lp_hbm, lp_ref),
                (root_len_hbm, root_len),
                (mid_len_hbm, mid_len),
                (mid_parent_hbm, mid_parent),
            )
        )
    ]
    second = [
        pltpu.make_async_copy(src, dst, loc_sem.at[12 + i])
        for i, (src, dst) in enumerate(((fk_hbm, fk_ref), (fv_hbm, fv_ref), (leaf_len_hbm, leaf_len)))
    ]
    late = [
        pltpu.make_async_copy(src, dst, loc_sem.at[15 + i])
        for i, (src, dst) in enumerate(
            (
                (ids_hbm, ids_ref),
                (gw_hbm, gw_ref),
                (resid_hbm.at[pl.ds(pl.multiple_of(c * 16, 16), 16)], resid_ref),
                (ow_hbm, ow_ref),
                (gain_hbm, gain_ref),
            )
        )
    ]
    for cp in stage:
        cp.start()
    for cp in early + second:
        cp.start()
    leaf_k.start()
    leaf_v.start()
    for cp in late:
        cp.start()
    load_gu.start()
    load_dn.start()

    barrier = pltpu.get_barrier_semaphore()

    def greet(i, carry):
        pl.semaphore_signal(barrier, inc=1, device_id=(r, row_mate(i)), device_id_type=MESH)
        pl.semaphore_signal(barrier, inc=1, device_id=(col_mate(i), c), device_id_type=MESH)
        return carry

    lax.fori_loop(1, N, greet, 0)
    load_q.wait()
    row = q_in[...].astype(F32)
    for h in range(32):
        q_rows[h : h + 1, :] = row[:, h * HEAD : (h + 1) * HEAD]
    q_ref[...] = q_rows[...].astype(BF16).reshape(4, 8, HEAD)
    for cp in early:
        cp.wait()

    lp = lp_ref[...]
    root_of = jnp.zeros((1, TOKENS), jnp.int32)
    for m in range(MIDS):
        root_of = jnp.where(lp == m, mid_parent[m], root_of)
    slot16 = iota((16, 1), 0)
    slot8 = jnp.bitwise_and(slot16, 7)
    of_core = jnp.where(slot16 < 8, core, 1 - core)
    far = jnp.where(slot8 == 6, 6, 2)
    from_z = lax.rem(
        z + jnp.where(slot8 < 2, 0, jnp.where(slot8 < 4, 7, jnp.where(slot8 < 6, 1, far))), 8
    )
    page_of = jnp.where(slot8 < 6, jnp.bitwise_and(slot8, 1), slot8 - 6)
    page_id = 2 * (r * N + 2 * from_z + of_core) + page_of
    place = jnp.sum(
        jnp.where(pt_ref[...] == page_id, iota((16, 512), 1), 0).astype(F32), axis=1, keepdims=True
    ).astype(jnp.int32)
    owner = jnp.zeros((16, 1), jnp.int32)
    first = jnp.zeros((16, 1), jnp.int32)
    length = jnp.zeros((16, 1), jnp.int32)
    root_slots = ROOTS * ROOT_PAGES
    for m in range(ROOTS):
        hit = (place >= m * ROOT_PAGES) & (place < (m + 1) * ROOT_PAGES)
        owner = jnp.where(hit, m, owner)
        first = jnp.where(hit, m * ROOT_PAGES, first)
        length = jnp.where(hit, root_len[m], length)
    for m in range(MIDS):
        lo = root_slots + m * MID_PAGES
        hit = (place >= lo) & (place < lo + MID_PAGES)
        owner = jnp.where(hit, m, owner)
        first = jnp.where(hit, lo, first)
        length = jnp.where(hit, mid_len[m], length)
    alive = length - (place - first) * HEAD
    owned = jnp.where(place < root_slots, root_of, lp) == owner
    missing = jnp.concatenate(
        [jnp.where(owned, 0.0, 1.0), jnp.ones((1, TOKENS), F32), jnp.zeros((111, TOKENS), F32)], axis=0
    )
    feat[...] = (missing.T * DEAD).astype(BF16)
    lane = iota((128, 128), 1)
    for p in range(16):
        limit = jnp.broadcast_to(alive[p : p + 1, :], (128, 128))
        dead = jnp.where(iota((128, 128), 0) < limit, 0.0, 1.0)
        kfeat[p] = jnp.where(lane == p, 1.0, jnp.where(lane == 16, dead, 0.0)).astype(BF16)

    def spread(b, carry):
        some = feat[pl.ds(pl.multiple_of(b * 16, 16), 16), :]
        for g in range(4):
            qfeat[b, g * 16 : (g + 1) * 16, :] = some
        return carry

    lax.fori_loop(0, N, spread, 0)

    for cp in second:
        cp.wait()
    leaf_k.wait()
    leaf_v.wait()
    for k in range(4):
        q8 = q_ref[k]
        s = dot_nt(q8, ownk[0, :, k * HEAD : (k + 1) * HEAD])
        s = jnp.where(iota((8, 512), 1) < leaf_len[0], s, DEAD)
        fresh = jnp.sum(q8.astype(F32) * fk_ref[:, k * HEAD : (k + 1) * HEAD].astype(F32), axis=1, keepdims=True)
        m = jnp.maximum(jnp.max(s, axis=1, keepdims=True), fresh)
        p = jnp.exp2((s - m) * SCORE)
        pf = jnp.exp2((fresh - m) * SCORE)
        total = jnp.sum(p, axis=1, keepdims=True) + pf
        acc = dot(p.astype(BF16), ownv[0, :, k * HEAD : (k + 1) * HEAD]) + pf * fv_ref[:, k * HEAD : (k + 1) * HEAD].astype(F32)
        m = jnp.broadcast_to(m, (8, HEAD))
        total = jnp.broadcast_to(total, (8, HEAD))
        for j in range(4):
            two = slice(2 * j, 2 * j + 2)
            lsend[4 * k + j] = jnp.concatenate([acc[two], m[two], total[two], total[two]], axis=0)

    for cp in stage:
        cp.wait()
    pl.semaphore_wait(barrier, 2 * (N - 1))

    def q1_copy(i):
        to = row_mate(i)
        head = lax.rem(to // 2, 4)
        return remote(q_ref.at[head], q1buf.at[c], q1_s.at[0], q1_r.at[0], (r, to))

    def q1_start(i, carry):
        q1_copy(i).start()
        return carry

    lax.fori_loop(1, N, q1_start, 0)

    def kv_copies():
        out = []
        for which, (src, dst) in enumerate(((kst, kraw), (vst, vbuf))):
            for step, first, pages, slot in ((1, 0, 2, 2), (7, 0, 2, 4), (2, 0, 1, 6), (6, 1, 1, 7)):
                zt = lax.rem(z + step, 8)
                out.append(
                    remote(
                        src.at[lax.rem(zt, 4), pl.ds(first, pages)],
                        dst.at[pl.ds(slot, pages)],
                        kv_s.at[which],
                        kv_r.at[which],
                        (r, zt * 2 + core),
                    )
                )
        return out

    kv_list = kv_copies()
    for cp in kv_list:
        cp.start()
    sibling = (r, c + 1 - 2 * core)
    own_fw = [
        remote(src.at[kv], dst.at[pl.ds(8, 2)], fw_s.at[which], fw_r.at[which], sibling)
        for which, (src, dst) in enumerate(((kst, kraw), (vst, vbuf)))
    ]
    for cp in own_fw:
        cp.start()
    q1buf[c] = q_ref[kv]

    all_here(q1buf, q1_r.at[0])
    order = jnp.where(
        iota((64, 128), 1) == lax.rem(iota((64, 128), 0), N) * 8 + 4 * core + iota((64, 128), 0) // N, 1.0, 0.0
    ).astype(BF16)
    qblk[r] = dot(order, q1buf[...].reshape(128, HEAD)).astype(BF16)

    def q2_copy(i):
        to = col_mate(i)
        return remote(qblk.at[r], qblk.at[r], q2_s.at[0], q2_r.at[r], (to, c))

    def q2_start(i, carry):
        q2_copy(i).start()
        return carry

    lax.fori_loop(1, N, q2_start, 0)

    def leaf_copy(i):
        to = row_mate(i)
        return remote(lsend.at[to], lrecv.at[c], lf_s.at[0], lf_r.at[0], (r, to))

    def leaf_start(i, carry):
        leaf_copy(i).start()
        return carry

    lax.fori_loop(1, N, leaf_start, 0)
    lrecv[c] = lsend[c]

    for which, buf in enumerate((kraw, vbuf)):
        six = buf.at[pl.ds(2, 6)]
        pltpu.make_async_copy(six, six, kv_r.at[which]).wait()
        remote(six, buf.at[pl.ds(10, 6)], fw_s.at[which], fw_r.at[which], sibling).start()
    kraw[0:2] = kst[kv]
    vbuf[0:2] = vst[kv]
    for p in range(8):
        vt[:, p * 128 : (p + 1) * 128] = vbuf[p].astype(F32).T.astype(BF16)
    for which, buf in enumerate((kraw, vbuf)):
        eight = buf.at[pl.ds(8, 8)]
        pltpu.make_async_copy(eight, eight, fw_r.at[which]).wait()
    for p in range(8, 16):
        vt[:, p * 128 : (p + 1) * 128] = vbuf[p].astype(F32).T.astype(BF16)

    def acc_copy(b):
        return remote(sacc.at[b], racc.at[r], ac_s.at[0], ac_r.at[0], (b, c))

    def attend(i, carry):
        four = lax.rem(r // 4 + i, N // 4)
        blocks = tuple(4 * four + n for n in range(4))
        for b in blocks:

            @pl.when(b != r)
            def _():
                remote(qblk.at[r], qblk.at[b], q2_s.at[0], q2_r.at[b], (b, c)).wait_recv()

        keys = jnp.concatenate([kraw[...].reshape(2048, HEAD), kfeat[...].reshape(2048, 128)], axis=1)
        q = jnp.concatenate([jnp.concatenate([qblk[b], qfeat[b]], axis=1) for b in blocks], axis=0)
        s = dot_nt(keys, q)
        m = jnp.max(s, axis=0, keepdims=True).astype(BF16).astype(F32)
        p = jnp.exp2((s - m) * SCORE)
        total = jnp.sum(p, axis=0, keepdims=True)
        acc = dot(vt[...], p.astype(BF16)).T.astype(BF16)
        hi = total.astype(BF16).astype(F32)
        row = iota((16, 256), 0)
        tail = jnp.where(row == 0, m, jnp.where(row == 1, hi, jnp.where(row == 2, total - hi, 0.0)))
        tail = tail.astype(BF16)
        for n, b in enumerate(blocks):
            sacc[b, 0:64, :] = acc[n * 64 : (n + 1) * 64, :]
            sacc[b, 64:80, :] = tail[:, n // 2 * 128 : (n // 2 + 1) * 128]

            @pl.when(b != r)
            def _():
                acc_copy(b).start()

        return carry

    lax.fori_loop(0, N // 4, attend, 0)

    for cp in late:
        cp.wait()
    ids = ids_ref[...]
    gw = gw_ref[...]
    chosen, weight = [], []
    for e in range(EXPERTS_HERE):
        hit = ids == c * EXPERTS_HERE + e
        chosen.append(jnp.max(jnp.where(hit, 1.0, 0.0), axis=0, keepdims=True))
        weight.append(jnp.sum(jnp.where(hit, gw, 0.0), axis=0, keepdims=True))
    picks = jnp.concatenate(chosen, axis=0)
    upto = jnp.where(iota((TOKENS, TOKENS), 0) <= iota((TOKENS, TOKENS), 1), 1.0, 0.0).astype(BF16)
    rank = dot(picks.astype(BF16), upto) - 1.0
    for e in range(EXPERTS_HERE):
        slot = iota((CAP, TOKENS), 0).astype(F32)
        one = jnp.where((rank[e : e + 1, :] == slot) & (picks[e : e + 1, :] > 0.5), 1.0, 0.0)
        disp[e * CAP : (e + 1) * CAP, :] = one.astype(BF16)
        slotw[e * CAP : (e + 1) * CAP, :] = jnp.broadcast_to(
            jnp.sum(one * weight[e], axis=1, keepdims=True), (CAP, 128)
        )
    dispt[...] = disp[...].astype(F32).T.astype(BF16)

    racc[r] = sacc[r]

    all_here(racc, ac_r.at[0])
    tails = racc[:, 64:80, :].astype(F32)
    top = jnp.max(tails[:, 0, :], axis=0, keepdims=True)
    scale = jnp.exp2((tails[:, 0, :] - top) * SCORE)
    total = jnp.sum(scale * (tails[:, 1, :] + tails[:, 2, :]), axis=0, keepdims=True)
    hi = total.astype(BF16).astype(F32)
    turned[...] = jnp.concatenate([scale, top, hi, total - hi, jnp.zeros((109, 128), F32)], axis=0).T
    tail = turned[pl.ds(pl.multiple_of(64 * lax.rem(r, 2), 64), 64), :]
    acc = racc[0, 0:64, :].astype(F32) * tail[:, 0:1]
    for i in range(1, N):
        acc = acc + racc[i, 0:64, :].astype(F32) * tail[:, i : i + 1]
    msg[:, :, 0:128] = acc.astype(BF16).reshape(2, 32, 128)
    msg[:, :, 128:256] = tail.astype(BF16).reshape(2, 32, 128)
    here = z // 4

    for j in range(2):
        to = 4 * kv + 2 * core + j

        @pl.when(to != c)
        def _():
            remote(msg.at[j], rmsg.at[here], ms_s.at[j], ms_r.at[0], (r, to)).start()

        @pl.when(to == c)
        def _():
            pltpu.make_async_copy(msg.at[j], rmsg.at[here], ms_r.at[0]).start()

    all_here(lrecv, lf_r.at[0])
    leaf_acc = jnp.concatenate([lrecv[:, 0, :], lrecv[:, 1, :]], axis=0)
    leaf_m = jnp.concatenate([lrecv[:, 2, :], lrecv[:, 3, :]], axis=0)
    leaf_t = jnp.concatenate([lrecv[:, 4, :], lrecv[:, 5, :]], axis=0)
    pltpu.make_async_copy(msg, rmsg, ms_r.at[0]).wait()
    parts = []
    top = leaf_m
    for s in range(2):
        tail = rmsg[s, :, 128:256].astype(F32)
        m = jnp.broadcast_to(tail[:, 16:17], (32, 128))
        parts.append((m, tail[:, 17:18] + tail[:, 18:19], rmsg[s, :, 0:128].astype(F32)))
        top = jnp.maximum(top, m)
    f = jnp.exp2((leaf_m - top) * SCORE)
    acc, total = leaf_acc * f, leaf_t * f
    for m, t, a in parts:
        f = jnp.exp2((m - top) * SCORE)
        acc = acc + a * f
        total = total + t * f
    attnb[r] = (acc / total).astype(BF16)

    def an_copy(i):
        return remote(attnb.at[r], attnb.at[r], an_s.at[0], an_r.at[0], (col_mate(i), c))

    def an_start(i, carry):
        an_copy(i).start()
        return carry

    lax.fori_loop(1, N, an_start, 0)
    all_here(attnb, an_r.at[0])

    proj = dot(attnb[:, 0:16, :].reshape(TOKENS, HEAD), ow_ref[0:HEAD, :])
    proj = proj + dot(attnb[:, 16:32, :].reshape(TOKENS, HEAD), ow_ref[HEAD : 2 * HEAD, :])
    psend[...] = proj.astype(BF16).reshape(N, 16, 128)

    def pr_copy(i):
        to = row_mate(i)
        return remote(psend.at[to], precv.at[c], pr_s.at[0], pr_r.at[0], (r, to))

    def pr_start(i, carry):
        pr_copy(i).start()
        return carry

    lax.fori_loop(1, N, pr_start, 0)
    precv[c] = psend[c]
    all_here(precv, pr_r.at[0])
    own_att = resid_ref[...].astype(F32) + jnp.sum(precv[...].astype(F32), axis=0)
    attb[c] = own_att.astype(BF16)

    def at_copy(i):
        to = row_mate(i)
        return remote(attb.at[c], attb.at[c], at_s.at[0], at_r.at[0], (r, to))

    def at_start(i, carry):
        at_copy(i).start()
        return carry

    lax.fori_loop(1, N, at_start, 0)

    all_here(attb, at_r.at[0])
    att = attb[...].reshape(TOKENS, 128)
    att_ref[...] = att

    wide = att.astype(F32)
    squares = jnp.sum(wide * wide, axis=1, keepdims=True)
    hi = squares.astype(BF16).astype(F32)
    lane = iota((TOKENS, 128), 1)
    side = jnp.where(lane == 0, hi, jnp.where(lane == 1, squares - hi, 0.0))
    scaled = (wide * gain_ref[...]).astype(BF16)
    rin[...] = dot(disp[...], jnp.concatenate([scaled, side.astype(BF16)], axis=1)).astype(BF16)
    load_gu.wait()

    def gu_copy(to):
        return remote(gsend.at[to], grecv.at[r], gu_s.at[0], gu_r.at[0], (to, c))

    def gate_up(i, carry):
        e = lax.rem(r // 2 + 4 + i, EXPERTS_HERE)
        rows = rin[pl.ds(pl.multiple_of(e * CAP, CAP), CAP), :]
        part = dot(rows[:, 0:128], wgu[e]).astype(BF16)
        for half in range(2):
            to = 2 * e + half
            cut = slice(16 * half, 16 * half + 16)
            gsend[to, :, 0 : 2 * FFE] = part[cut, :]
            gsend[to, :, 2 * FFE : WIDE] = rows[cut, 128:256]

            @pl.when(to != r)
            def _():
                gu_copy(to).start()

        return carry

    lax.fori_loop(0, EXPERTS_HERE, gate_up, 0)
    grecv[r] = gsend[r]

    all_here(grecv, gu_r.at[0])

    def gu_add(i, acc):
        return acc + grecv[i].astype(F32)

    gu = lax.fori_loop(0, N, gu_add, jnp.zeros((16, WIDE), F32))
    inverse = lax.rsqrt((gu[:, 2 * FFE : 2 * FFE + 1] + gu[:, 2 * FFE + 1 : 2 * FFE + 2]) / D + EPS)
    gate = gu[:, 0:FFE] * inverse
    up = gu[:, FFE : 2 * FFE] * inverse
    actb[r] = (gate / (1.0 + jnp.exp(-gate)) * up).astype(BF16)

    def av_copy(i):
        to = col_mate(i)
        return remote(actb.at[r], actb.at[r], av_s.at[0], av_r.at[r], (to, c))

    def av_start(i, carry):
        av_copy(i).start()
        return carry

    lax.fori_loop(1, N, av_start, 0)
    load_dn.wait()


    def down(i, carry):
        e = lax.rem(r // 2 + i, EXPERTS_HERE)
        for src in (2 * e, 2 * e + 1):

            @pl.when(src != r)
            def _():
                remote(actb.at[r], actb.at[src], av_s.at[0], av_r.at[src], (src, c)).wait_recv()

        rows = actb[pl.ds(2 * e, 2)].reshape(CAP, FFE)
        at = pl.ds(pl.multiple_of(e * CAP, CAP), CAP)
        y = dot(rows, wdn[e]) * slotw[at, :]
        hi = y.astype(BF16)
        yb[at, 0:128] = hi
        yb[at, 128:256] = (y - hi.astype(F32)).astype(BF16)
        return carry

    lax.fori_loop(0, EXPERTS_HERE, down, 0)
    mixed = dot(dispt[...], yb[...])
    msend[...] = (mixed[:, 0:128] + mixed[:, 128:256]).astype(BF16).reshape(N, 16, 128)

    def mx_copy(i):
        to = row_mate(i)
        return remote(msend.at[to], mrecv.at[c], mx_s.at[0], mx_r.at[0], (r, to))

    def mx_start(i, carry):
        mx_copy(i).start()
        return carry

    lax.fori_loop(1, N, mx_start, 0)
    mrecv[c] = msend[c]

    all_here(mrecv, mx_r.at[0])
    lay_ref[...] = (attb[c].astype(F32) + jnp.sum(mrecv[...].astype(F32), axis=0)).astype(BF16)

    for which, buf in enumerate((kraw, vbuf)):
        six = buf.at[pl.ds(2, 6)]
        pltpu.make_async_copy(six, six, kv_s.at[which]).wait()
    for which, buf in enumerate((kraw, vbuf)):
        eight = buf.at[pl.ds(8, 8)]
        pltpu.make_async_copy(eight, eight, fw_s.at[which]).wait()
    all_here(q1buf, q1_s.at[0])
    all_here(qblk, q2_s.at[0])
    all_here(lsend, lf_s.at[0])
    all_here(sacc, ac_s.at[0])
    all_here(attnb, an_s.at[0])
    all_here(psend, pr_s.at[0])
    all_here(attb, at_s.at[0])
    all_here(gsend, gu_s.at[0])
    all_here(actb, av_s.at[0])
    all_here(msend, mx_s.at[0])
    for j in range(2):
        to = 4 * kv + 2 * core + j

        @pl.when(to != c)
        def _():
            remote(msg.at[j], rmsg.at[here], ms_s.at[j], ms_r.at[0], (r, to)).wait_send()


def per_device(
    fresh_queries,
    fresh_key,
    fresh_value,
    request_own_keys,
    request_own_values,
    leaf_len,
    prefix_pool_keys,
    prefix_pool_values,
    page_table,
    root_len,
    mid_len,
    mid_parent,
    leaf_parent,
    residual,
    out_weight,
    post_gain,
    expert_ids,
    gate_weight,
    w_gate_up,
    w_down,
):
    vmem = pl.BlockSpec(memory_space=pltpu.VMEM)
    hbm = pl.BlockSpec(memory_space=pltpu.HBM)
    dma = lambda n: pltpu.SemaphoreType.DMA((n,))
    return pl.pallas_call(
        kernel,
        out_shape=(
            jax.ShapeDtypeStruct((TOKENS, 128), BF16),
            jax.ShapeDtypeStruct((16, 128), BF16),
        ),
        in_specs=[hbm] * 20,
        out_specs=(vmem, vmem),
        scratch_shapes=[
            pltpu.VMEM((1, 4096), BF16),
            pltpu.VMEM((1, 512), BF16),
            pltpu.VMEM((1, 512), BF16),
            pltpu.VMEM((1, 512), jnp.int32),
            pltpu.VMEM((1, TOKENS), jnp.int32),
            pltpu.VMEM((16, 128), BF16),
            pltpu.VMEM((TOKENS, 128), BF16),
            pltpu.VMEM((1, 128), F32),
            pltpu.VMEM((8, TOKENS), jnp.int32),
            pltpu.VMEM((8, TOKENS), F32),
            pltpu.SMEM((1,), jnp.int32),
            pltpu.SMEM((ROOTS,), jnp.int32),
            pltpu.SMEM((MIDS,), jnp.int32),
            pltpu.SMEM((MIDS,), jnp.int32),
            pltpu.VMEM((32, HEAD), F32),
            pltpu.VMEM((4, 8, HEAD), BF16),
            pltpu.VMEM((1, 512, 512), BF16),
            pltpu.VMEM((1, 512, 512), BF16),
            pltpu.VMEM((EXPERTS_HERE, 128, 2 * FFE), BF16),
            pltpu.VMEM((EXPERTS_HERE, FFE, 128), BF16),
            pltpu.VMEM((4, 2, 128, HEAD), BF16),
            pltpu.VMEM((4, 2, 128, HEAD), BF16),
            pltpu.VMEM((16, 128, HEAD), BF16),
            pltpu.VMEM((16, 128, 128), BF16),
            pltpu.VMEM((16, 128, HEAD), BF16),
            pltpu.VMEM((HEAD, 2048), BF16),
            pltpu.VMEM((TOKENS, 128), BF16),
            pltpu.VMEM((N, 64, 128), BF16),
            pltpu.VMEM((N, 8, HEAD), BF16),
            pltpu.VMEM((N, 64, HEAD), BF16),
            pltpu.VMEM((N, 80, 128), BF16),
            pltpu.VMEM((N, 80, 128), BF16),
            pltpu.VMEM((128, 128), F32),
            pltpu.VMEM((2, 32, 256), BF16),
            pltpu.VMEM((2, 32, 256), BF16),
            pltpu.VMEM((N, 8, 128), F32),
            pltpu.VMEM((N, 8, 128), F32),
            pltpu.VMEM((N, 32, 128), BF16),
            pltpu.VMEM((N, 16, 128), BF16),
            pltpu.VMEM((N, 16, 128), BF16),
            pltpu.VMEM((N, 16, 128), BF16),
            pltpu.VMEM((TOKENS, TOKENS), BF16),
            pltpu.VMEM((TOKENS, TOKENS), BF16),
            pltpu.VMEM((TOKENS, 128), F32),
            pltpu.VMEM((TOKENS, 256), BF16),
            pltpu.VMEM((N, 16, WIDE), BF16),
            pltpu.VMEM((N, 16, WIDE), BF16),
            pltpu.VMEM((N, 16, FFE), BF16),
            pltpu.VMEM((TOKENS, 256), BF16),
            pltpu.VMEM((N, 16, 128), BF16),
            pltpu.VMEM((N, 16, 128), BF16),
            dma(28),
            dma(2), dma(2),
            dma(2), dma(2),
            dma(1), dma(1),
            dma(1), dma(N),
            dma(1), dma(1),
            dma(4), dma(1),
            dma(1), dma(1),
            dma(1), dma(1),
            dma(1), dma(1),
            dma(1), dma(1),
            dma(1), dma(1),
            dma(1), dma(N),
            dma(1), dma(1),
        ],
        compiler_params=pltpu.CompilerParams(
            collective_id=0, has_side_effects=True
        ),
    )(
        fresh_queries,
        fresh_key,
        fresh_value,
        request_own_keys,
        request_own_values,
        leaf_len,
        prefix_pool_keys,
        prefix_pool_values,
        page_table.reshape(1, 512),
        root_len,
        mid_len,
        mid_parent,
        leaf_parent.reshape(1, TOKENS),
        residual,
        out_weight,
        post_gain.reshape(1, 128),
        expert_ids.T,
        gate_weight.T,
        w_gate_up,
        w_down,
    )


def solution(mesh):
    placed = (
        P(("row", "col"), None),
        P(("row", "col"), None),
        P(("row", "col"), None),
        P(("row", "col"), None, None),
        P(("row", "col"), None, None),
        P(("row", "col")),
        P(("row", "col"), None, None),
        P(("row", "col"), None, None),
        P(),
        P(),
        P(),
        P(),
        P(),
        P(None, "row"),
        P("col", "row"),
        P("row"),
        P(),
        P(),
        P("col", "row", None),
        P("col", None, "row"),
    )
    return jax.shard_map(
        per_device,
        mesh=mesh,
        in_specs=placed,
        out_specs=(P(None, "row"), P("col", "row")),
        check_vma=False,
    )
```

```python
import functools
import math

import jax
import jax.numpy as jnp
from jax import lax
from jax.experimental import pallas as pl
from jax.experimental.pallas import tpu as pltpu
from jax.sharding import PartitionSpec as P

D = 2048
HEAD = 128
FFE = 768
ROOTS = 4
MIDS = 32
ROOT_PAGES = 32
MID_PAGES = 12
N = 16
TOKENS = 256
CAP = 32
EXPERTS_HERE = 8
WIDE = 2 * FFE + 128
EPS = 1e-06
DEAD = -float(2**99)
LOG2E = math.log2(math.e)
SCORE = LOG2E / math.sqrt(HEAD)
MESH = pl.DeviceIdType.MESH
F32 = jnp.float32
BF16 = jnp.bfloat16


def dot(a, b):
    return jnp.dot(a, b, preferred_element_type=F32)


def dot_nt(a, b):
    return lax.dot_general(a, b, (((1,), (1,)), ((), ())), preferred_element_type=F32)


def iota(shape, axis):
    return lax.broadcasted_iota(jnp.int32, shape, axis)


def kernel(
    q_hbm,
    fk_hbm,
    fv_hbm,
    ownk_hbm,
    ownv_hbm,
    leaf_len_hbm,
    pk_hbm,
    pv_hbm,
    pt_hbm,
    root_len_hbm,
    mid_len_hbm,
    mid_parent_hbm,
    lp_hbm,
    resid_hbm,
    ow_hbm,
    gain_hbm,
    ids_hbm,
    gw_hbm,
    wgu_hbm,
    wdn_hbm,
    att_ref,
    lay_ref,
    q_in,
    fk_ref,
    fv_ref,
    pt_ref,
    lp_ref,
    resid_ref,
    ow_ref,
    gain_ref,
    ids_ref,
    gw_ref,
    leaf_len,
    root_len,
    mid_len,
    mid_parent,
    q_rows,
    q_ref,
    ownk,
    ownv,
    wgu,
    wdn,
    kst,
    vst,
    kraw,
    kfeat,
    vbuf,
    vt,
    feat,
    qfeat,
    q1buf,
    qblk,
    sacc,
    racc,
    turned,
    msg,
    rmsg,
    lsend,
    lrecv,
    attnb,
    psend,
    precv,
    attb,
    disp,
    dispt,
    slotw,
    rin,
    gsend,
    grecv,
    actb,
    yb,
    msend,
    mrecv,
    loc_sem,
    kv_s,
    kv_r,
    fw_s,
    fw_r,
    q1_s,
    q1_r,
    q2_s,
    q2_r,
    ac_s,
    ac_r,
    ms_s,
    ms_r,
    lf_s,
    lf_r,
    an_s,
    an_r,
    pr_s,
    pr_r,
    at_s,
    at_r,
    gu_s,
    gu_r,
    av_s,
    av_r,
    mx_s,
    mx_r,
):
    r = lax.axis_index("row")
    c = lax.axis_index("col")
    z = c // 2
    core = lax.rem(c, 2)
    kv = lax.rem(z, 4)

    def remote(src, dst, ssem, rsem, dev):
        return pltpu.make_async_remote_copy(
            src_ref=src, dst_ref=dst, send_sem=ssem, recv_sem=rsem, device_id=dev, device_id_type=MESH
        )

    def all_here(buf, sem):
        block = buf.at[pl.ds(0, N - 1)]
        pltpu.make_async_copy(block, block, sem).wait()

    def row_mate(i):
        return lax.rem(c + N // 2 + (1 - 2 * lax.rem(i, 2)) * (i // 2), N)

    def col_mate(i):
        k = i - 1 + i // 11
        return lax.rem(r // 4 + k // 4 + 2, 4) * 4 + lax.rem(lax.rem(r, 4) + lax.rem(k, 4) + 2, 4)

    stage = [
        pltpu.make_async_copy(
            src.at[:, :, k * HEAD : (k + 1) * HEAD], dst.at[k], loc_sem.at[20 + which * 4 + k]
        )
        for which, (src, dst) in enumerate(((pk_hbm, kst), (pv_hbm, vst)))
        for k in range(4)
    ]
    leaf_k = pltpu.make_async_copy(ownk_hbm, ownk, loc_sem.at[2])
    leaf_v = pltpu.make_async_copy(ownv_hbm, ownv, loc_sem.at[3])
    load_gu = pltpu.make_async_copy(wgu_hbm, wgu, loc_sem.at[4])
    load_dn = pltpu.make_async_copy(wdn_hbm, wdn, loc_sem.at[5])
    load_q = pltpu.make_async_copy(q_hbm, q_in, loc_sem.at[6])
    load_q.start()
    early = [
        pltpu.make_async_copy(src, dst, loc_sem.at[7 + i])
        for i, (src, dst) in enumerate(
            (
                (pt_hbm, pt_ref),
                (lp_hbm, lp_ref),
                (root_len_hbm, root_len),
                (mid_len_hbm, mid_len),
                (mid_parent_hbm, mid_parent),
            )
        )
    ]
    second = [
        pltpu.make_async_copy(src, dst, loc_sem.at[12 + i])
        for i, (src, dst) in enumerate(((fk_hbm, fk_ref), (fv_hbm, fv_ref), (leaf_len_hbm, leaf_len)))
    ]
    late = [
        pltpu.make_async_copy(src, dst, loc_sem.at[15 + i])
        for i, (src, dst) in enumerate(
            (
                (ids_hbm, ids_ref),
                (gw_hbm, gw_ref),
                (resid_hbm.at[pl.ds(pl.multiple_of(c * 16, 16), 16)], resid_ref),
                (ow_hbm, ow_ref),
                (gain_hbm, gain_ref),
            )
        )
    ]
    for cp in stage:
        cp.start()
    for cp in early + second:
        cp.start()
    leaf_k.start()
    leaf_v.start()
    for cp in late:
        cp.start()
    load_gu.start()
    load_dn.start()

    barrier = pltpu.get_barrier_semaphore()

    def greet(i, carry):
        pl.semaphore_signal(barrier, inc=1, device_id=(r, row_mate(i)), device_id_type=MESH)
        pl.semaphore_signal(barrier, inc=1, device_id=(col_mate(i), c), device_id_type=MESH)
        return carry

    lax.fori_loop(1, N, greet, 0)
    load_q.wait()
    row = q_in[...].astype(F32)
    for h in range(32):
        q_rows[h : h + 1, :] = row[:, h * HEAD : (h + 1) * HEAD]
    q_ref[...] = q_rows[...].astype(BF16).reshape(4, 8, HEAD)
    for cp in early:
        cp.wait()

    lp = lp_ref[...]
    root_of = jnp.zeros((1, TOKENS), jnp.int32)
    for m in range(MIDS):
        root_of = jnp.where(lp == m, mid_parent[m], root_of)
    slot16 = iota((16, 1), 0)
    slot8 = jnp.bitwise_and(slot16, 7)
    of_core = jnp.where(slot16 < 8, core, 1 - core)
    far = jnp.where(slot8 == 6, 6, 2)
    from_z = lax.rem(
        z + jnp.where(slot8 < 2, 0, jnp.where(slot8 < 4, 7, jnp.where(slot8 < 6, 1, far))), 8
    )
    page_of = jnp.where(slot8 < 6, jnp.bitwise_and(slot8, 1), slot8 - 6)
    page_id = 2 * (r * N + 2 * from_z + of_core) + page_of
    place = jnp.sum(
        jnp.where(pt_ref[...] == page_id, iota((16, 512), 1), 0).astype(F32), axis=1, keepdims=True
    ).astype(jnp.int32)
    owner = jnp.zeros((16, 1), jnp.int32)
    first = jnp.zeros((16, 1), jnp.int32)
    length = jnp.zeros((16, 1), jnp.int32)
    root_slots = ROOTS * ROOT_PAGES
    for m in range(ROOTS):
        hit = (place >= m * ROOT_PAGES) & (place < (m + 1) * ROOT_PAGES)
        owner = jnp.where(hit, m, owner)
        first = jnp.where(hit, m * ROOT_PAGES, first)
        length = jnp.where(hit, root_len[m], length)
    for m in range(MIDS):
        lo = root_slots + m * MID_PAGES
        hit = (place >= lo) & (place < lo + MID_PAGES)
        owner = jnp.where(hit, m, owner)
        first = jnp.where(hit, lo, first)
        length = jnp.where(hit, mid_len[m], length)
    alive = length - (place - first) * HEAD
    owned = jnp.where(place < root_slots, root_of, lp) == owner
    missing = jnp.concatenate(
        [jnp.where(owned, 0.0, 1.0), jnp.ones((1, TOKENS), F32), jnp.zeros((111, TOKENS), F32)], axis=0
    )
    feat[...] = (missing.T * DEAD).astype(BF16)
    lane = iota((128, 128), 1)
    for p in range(16):
        limit = jnp.broadcast_to(alive[p : p + 1, :], (128, 128))
        dead = jnp.where(iota((128, 128), 0) < limit, 0.0, 1.0)
        kfeat[p] = jnp.where(lane == p, 1.0, jnp.where(lane == 16, dead, 0.0)).astype(BF16)

    def spread(b, carry):
        some = feat[pl.ds(pl.multiple_of(b * 16, 16), 16), :]
        for g in range(4):
            qfeat[b, g * 16 : (g + 1) * 16, :] = some
        return carry

    lax.fori_loop(0, N, spread, 0)

    for cp in stage:
        cp.wait()
    kraw[0:2] = kst[kv]
    vbuf[0:2] = vst[kv]

    def turn(first, last):
        for p in range(first, last):
            vt[:, p * 128 : (p + 1) * 128] = vbuf[p].astype(F32).T.astype(BF16)

    turn(0, 2)
    pl.semaphore_wait(barrier, 2 * (N - 1))

    def q1_copy(i):
        to = row_mate(i)
        head = lax.rem(to // 2, 4)
        return remote(q_ref.at[head], q1buf.at[c], q1_s.at[0], q1_r.at[0], (r, to))

    def q1_start(i, carry):
        q1_copy(i).start()
        return carry

    lax.fori_loop(1, N, q1_start, 0)

    def kv_copies():
        out = []
        for which, (src, dst) in enumerate(((kst, kraw), (vst, vbuf))):
            for step, first, pages, slot in ((1, 0, 2, 2), (7, 0, 2, 4), (2, 0, 1, 6), (6, 1, 1, 7)):
                zt = lax.rem(z + step, 8)
                out.append(
                    remote(
                        src.at[lax.rem(zt, 4), pl.ds(first, pages)],
                        dst.at[pl.ds(slot, pages)],
                        kv_s.at[which],
                        kv_r.at[2 * which + slot // 6],
                        (r, zt * 2 + core),
                    )
                )
        return out

    kv_list = kv_copies()
    for cp in kv_list:
        cp.start()
    sibling = (r, c + 1 - 2 * core)
    own_fw = [
        remote(src.at[kv], dst.at[pl.ds(8, 2)], fw_s.at[which], fw_r.at[which], sibling)
        for which, (src, dst) in enumerate(((kst, kraw), (vst, vbuf)))
    ]
    for cp in own_fw:
        cp.start()
    q1buf[c] = q_ref[kv]

    all_here(q1buf, q1_r.at[0])
    order = jnp.where(
        iota((64, 128), 1) == lax.rem(iota((64, 128), 0), N) * 8 + 4 * core + iota((64, 128), 0) // N, 1.0, 0.0
    ).astype(BF16)
    qblk[r] = dot(order, q1buf[...].reshape(128, HEAD)).astype(BF16)

    def q2_copy(i):
        to = col_mate(i)
        return remote(qblk.at[r], qblk.at[r], q2_s.at[0], q2_r.at[r], (to, c))

    def q2_start(i, carry):
        q2_copy(i).start()
        return carry

    lax.fori_loop(1, N, q2_start, 0)

    for cp in second:
        cp.wait()
    leaf_k.wait()
    leaf_v.wait()
    for k in range(4):
        q8 = q_ref[k]
        s = dot_nt(q8, ownk[0, :, k * HEAD : (k + 1) * HEAD])
        s = jnp.where(iota((8, 512), 1) < leaf_len[0], s, DEAD)
        fresh = jnp.sum(q8.astype(F32) * fk_ref[:, k * HEAD : (k + 1) * HEAD].astype(F32), axis=1, keepdims=True)
        m = jnp.maximum(jnp.max(s, axis=1, keepdims=True), fresh)
        p = jnp.exp2((s - m) * SCORE)
        pf = jnp.exp2((fresh - m) * SCORE)
        total = jnp.sum(p, axis=1, keepdims=True) + pf
        acc = dot(p.astype(BF16), ownv[0, :, k * HEAD : (k + 1) * HEAD]) + pf * fv_ref[:, k * HEAD : (k + 1) * HEAD].astype(F32)
        m = jnp.broadcast_to(m, (8, HEAD))
        total = jnp.broadcast_to(total, (8, HEAD))
        for j in range(4):
            two = slice(2 * j, 2 * j + 2)
            lsend[4 * k + j] = jnp.concatenate([acc[two], m[two], total[two], total[two]], axis=0)

    def leaf_copy(i):
        to = row_mate(i)
        return remote(lsend.at[to], lrecv.at[c], lf_s.at[0], lf_r.at[0], (r, to))

    def leaf_start(i, carry):
        leaf_copy(i).start()
        return carry

    lax.fori_loop(1, N, leaf_start, 0)
    lrecv[c] = lsend[c]

    for far, (slot, pages) in enumerate(((2, 4), (6, 2))):
        for which, buf in enumerate((kraw, vbuf)):
            some = buf.at[pl.ds(slot, pages)]
            pltpu.make_async_copy(some, some, kv_r.at[2 * which + far]).wait()
            remote(some, buf.at[pl.ds(8 + slot, pages)], fw_s.at[which], fw_r.at[which], sibling).start()
        turn(slot, slot + pages)
    for which, buf in enumerate((kraw, vbuf)):
        eight = buf.at[pl.ds(8, 8)]
        pltpu.make_async_copy(eight, eight, fw_r.at[which]).wait()
    turn(8, 16)

    def acc_copy(b):
        return remote(sacc.at[b], racc.at[r], ac_s.at[0], ac_r.at[0], (b, c))

    def attend(i, carry):
        four = lax.rem(r // 4 + 1 + i, N // 4)
        blocks = tuple(4 * four + n for n in range(4))
        for b in blocks:

            @pl.when(b != r)
            def _():
                remote(qblk.at[r], qblk.at[b], q2_s.at[0], q2_r.at[b], (b, c)).wait_recv()

        keys = jnp.concatenate([kraw[...].reshape(2048, HEAD), kfeat[...].reshape(2048, 128)], axis=1)
        q = jnp.concatenate([jnp.concatenate([qblk[b], qfeat[b]], axis=1) for b in blocks], axis=0)
        s = dot_nt(keys, q)
        m = jnp.max(s, axis=0, keepdims=True).astype(BF16).astype(F32)
        p = jnp.exp2((s - m) * SCORE)
        total = jnp.sum(p, axis=0, keepdims=True)
        acc = dot(vt[...], p.astype(BF16)).T.astype(BF16)
        hi = total.astype(BF16).astype(F32)
        row = iota((16, 256), 0)
        tail = jnp.where(row == 0, m, jnp.where(row == 1, hi, jnp.where(row == 2, total - hi, 0.0)))
        tail = tail.astype(BF16)
        for n, b in enumerate(blocks):
            sacc[b, 0:64, :] = acc[n * 64 : (n + 1) * 64, :]
            sacc[b, 64:80, :] = tail[:, n // 2 * 128 : (n // 2 + 1) * 128]

            @pl.when(b != r)
            def _():
                acc_copy(b).start()

        return carry

    lax.fori_loop(0, N // 4, attend, 0)

    for cp in late:
        cp.wait()
    ids = ids_ref[...]
    gw = gw_ref[...]
    chosen, weight = [], []
    for e in range(EXPERTS_HERE):
        hit = ids == c * EXPERTS_HERE + e
        chosen.append(jnp.max(jnp.where(hit, 1.0, 0.0), axis=0, keepdims=True))
        weight.append(jnp.sum(jnp.where(hit, gw, 0.0), axis=0, keepdims=True))
    picks = jnp.concatenate(chosen, axis=0)
    upto = jnp.where(iota((TOKENS, TOKENS), 0) <= iota((TOKENS, TOKENS), 1), 1.0, 0.0).astype(BF16)
    rank = dot(picks.astype(BF16), upto) - 1.0
    for e in range(EXPERTS_HERE):
        slot = iota((CAP, TOKENS), 0).astype(F32)
        one = jnp.where((rank[e : e + 1, :] == slot) & (picks[e : e + 1, :] > 0.5), 1.0, 0.0)
        disp[e * CAP : (e + 1) * CAP, :] = one.astype(BF16)
        slotw[e * CAP : (e + 1) * CAP, :] = jnp.broadcast_to(
            jnp.sum(one * weight[e], axis=1, keepdims=True), (CAP, 128)
        )
    dispt[...] = disp[...].astype(F32).T.astype(BF16)

    racc[r] = sacc[r]

    all_here(racc, ac_r.at[0])
    tails = racc[:, 64:80, :].astype(F32)
    top = jnp.max(tails[:, 0, :], axis=0, keepdims=True)
    scale = jnp.exp2((tails[:, 0, :] - top) * SCORE)
    total = jnp.sum(scale * (tails[:, 1, :] + tails[:, 2, :]), axis=0, keepdims=True)
    hi = total.astype(BF16).astype(F32)
    turned[...] = jnp.concatenate([scale, top, hi, total - hi, jnp.zeros((109, 128), F32)], axis=0).T
    tail = turned[pl.ds(pl.multiple_of(64 * lax.rem(r, 2), 64), 64), :]
    acc = racc[0, 0:64, :].astype(F32) * tail[:, 0:1]
    for i in range(1, N):
        acc = acc + racc[i, 0:64, :].astype(F32) * tail[:, i : i + 1]
    msg[:, :, 0:128] = acc.astype(BF16).reshape(2, 32, 128)
    msg[:, :, 128:256] = tail.astype(BF16).reshape(2, 32, 128)
    here = z // 4

    for j in range(2):
        to = 4 * kv + 2 * core + j

        @pl.when(to != c)
        def _():
            remote(msg.at[j], rmsg.at[here], ms_s.at[j], ms_r.at[0], (r, to)).start()

        @pl.when(to == c)
        def _():
            pltpu.make_async_copy(msg.at[j], rmsg.at[here], ms_r.at[0]).start()

    all_here(lrecv, lf_r.at[0])
    leaf_acc = jnp.concatenate([lrecv[:, 0, :], lrecv[:, 1, :]], axis=0)
    leaf_m = jnp.concatenate([lrecv[:, 2, :], lrecv[:, 3, :]], axis=0)
    leaf_t = jnp.concatenate([lrecv[:, 4, :], lrecv[:, 5, :]], axis=0)
    pltpu.make_async_copy(msg, rmsg, ms_r.at[0]).wait()
    parts = []
    top = leaf_m
    for s in range(2):
        tail = rmsg[s, :, 128:256].astype(F32)
        m = jnp.broadcast_to(tail[:, 16:17], (32, 128))
        parts.append((m, tail[:, 17:18] + tail[:, 18:19], rmsg[s, :, 0:128].astype(F32)))
        top = jnp.maximum(top, m)
    f = jnp.exp2((leaf_m - top) * SCORE)
    acc, total = leaf_acc * f, leaf_t * f
    for m, t, a in parts:
        f = jnp.exp2((m - top) * SCORE)
        acc = acc + a * f
        total = total + t * f
    attnb[r] = (acc / total).astype(BF16)

    def an_copy(i):
        return remote(attnb.at[r], attnb.at[r], an_s.at[0], an_r.at[r], (col_mate(i), c))

    def an_start(i, carry):
        an_copy(i).start()
        return carry

    lax.fori_loop(1, N, an_start, 0)
    def pr_copy(b):
        return remote(psend.at[b], precv.at[c], pr_s.at[0], pr_r.at[0], (r, b))

    def project(b):
        both = attnb[b]
        psend[b] = dot(jnp.concatenate([both[0:16, :], both[16:32, :]], axis=1), ow_ref[...]).astype(BF16)

        @pl.when(b != c)
        def _():
            pr_copy(b).start()

    def project_next(i, carry):
        b = col_mate(N - i)
        remote(attnb.at[r], attnb.at[b], an_s.at[0], an_r.at[b], (b, c)).wait_recv()
        project(b)
        return carry

    project(r)
    lax.fori_loop(1, N, project_next, 0)
    precv[c] = psend[c]
    all_here(precv, pr_r.at[0])
    own_att = resid_ref[...].astype(F32) + jnp.sum(precv[...].astype(F32), axis=0)
    attb[c] = own_att.astype(BF16)

    def at_copy(i):
        to = row_mate(i)
        return remote(attb.at[c], attb.at[c], at_s.at[0], at_r.at[0], (r, to))

    def at_start(i, carry):
        at_copy(i).start()
        return carry

    lax.fori_loop(1, N, at_start, 0)

    all_here(attb, at_r.at[0])
    att = attb[...].reshape(TOKENS, 128)
    att_ref[...] = att

    wide = att.astype(F32)
    squares = jnp.sum(wide * wide, axis=1, keepdims=True)
    hi = squares.astype(BF16).astype(F32)
    lane = iota((TOKENS, 128), 1)
    side = jnp.where(lane == 0, hi, jnp.where(lane == 1, squares - hi, 0.0))
    scaled = (wide * gain_ref[...]).astype(BF16)
    rin[...] = dot(disp[...], jnp.concatenate([scaled, side.astype(BF16)], axis=1)).astype(BF16)
    load_gu.wait()

    def gu_copy(to):
        return remote(gsend.at[to], grecv.at[r], gu_s.at[0], gu_r.at[0], (to, c))

    def gate_up(i, carry):
        e = lax.rem(r // 2 + 4 + i, EXPERTS_HERE)
        rows = rin[pl.ds(pl.multiple_of(e * CAP, CAP), CAP), :]
        part = dot(rows[:, 0:128], wgu[e]).astype(BF16)
        for half in range(2):
            to = 2 * e + half
            cut = slice(16 * half, 16 * half + 16)
            gsend[to, :, 0 : 2 * FFE] = part[cut, :]
            gsend[to, :, 2 * FFE : WIDE] = rows[cut, 128:256]

            @pl.when(to != r)
            def _():
                gu_copy(to).start()

        return carry

    lax.fori_loop(0, EXPERTS_HERE, gate_up, 0)
    grecv[r] = gsend[r]

    all_here(grecv, gu_r.at[0])

    def gu_add(i, acc):
        return acc + grecv[i].astype(F32)

    gu = lax.fori_loop(0, N, gu_add, jnp.zeros((16, WIDE), F32))
    inverse = lax.rsqrt((gu[:, 2 * FFE : 2 * FFE + 1] + gu[:, 2 * FFE + 1 : 2 * FFE + 2]) / D + EPS)
    gate = gu[:, 0:FFE] * inverse
    up = gu[:, FFE : 2 * FFE] * inverse
    actb[r] = (gate / (1.0 + jnp.exp(-gate)) * up).astype(BF16)

    def av_copy(i):
        to = col_mate(i)
        return remote(actb.at[r], actb.at[r], av_s.at[0], av_r.at[r], (to, c))

    def av_start(i, carry):
        av_copy(i).start()
        return carry

    lax.fori_loop(1, N, av_start, 0)
    load_dn.wait()


    def down(i, carry):
        e = lax.rem(r // 2 + i, EXPERTS_HERE)
        for src in (2 * e, 2 * e + 1):

            @pl.when(src != r)
            def _():
                remote(actb.at[r], actb.at[src], av_s.at[0], av_r.at[src], (src, c)).wait_recv()

        rows = actb[pl.ds(2 * e, 2)].reshape(CAP, FFE)
        at = pl.ds(pl.multiple_of(e * CAP, CAP), CAP)
        y = dot(rows, wdn[e]) * slotw[at, :]
        hi = y.astype(BF16)
        yb[at, 0:128] = hi
        yb[at, 128:256] = (y - hi.astype(F32)).astype(BF16)
        return carry

    lax.fori_loop(0, EXPERTS_HERE, down, 0)
    mixed = dot(dispt[...], yb[...])
    msend[...] = (mixed[:, 0:128] + mixed[:, 128:256]).astype(BF16).reshape(N, 16, 128)

    def mx_copy(i):
        to = row_mate(i)
        return remote(msend.at[to], mrecv.at[c], mx_s.at[0], mx_r.at[0], (r, to))

    def mx_start(i, carry):
        mx_copy(i).start()
        return carry

    lax.fori_loop(1, N, mx_start, 0)
    mrecv[c] = msend[c]

    all_here(mrecv, mx_r.at[0])
    lay_ref[...] = (attb[c].astype(F32) + jnp.sum(mrecv[...].astype(F32), axis=0)).astype(BF16)

    for which, buf in enumerate((kraw, vbuf)):
        six = buf.at[pl.ds(2, 6)]
        pltpu.make_async_copy(six, six, kv_s.at[which]).wait()
    for which, buf in enumerate((kraw, vbuf)):
        eight = buf.at[pl.ds(8, 8)]
        pltpu.make_async_copy(eight, eight, fw_s.at[which]).wait()
    all_here(q1buf, q1_s.at[0])
    all_here(qblk, q2_s.at[0])
    all_here(lsend, lf_s.at[0])
    all_here(sacc, ac_s.at[0])
    all_here(attnb, an_s.at[0])
    all_here(psend, pr_s.at[0])
    all_here(attb, at_s.at[0])
    all_here(gsend, gu_s.at[0])
    all_here(actb, av_s.at[0])
    all_here(msend, mx_s.at[0])
    for j in range(2):
        to = 4 * kv + 2 * core + j

        @pl.when(to != c)
        def _():
            remote(msg.at[j], rmsg.at[here], ms_s.at[j], ms_r.at[0], (r, to)).wait_send()


def per_device(
    fresh_queries,
    fresh_key,
    fresh_value,
    request_own_keys,
    request_own_values,
    leaf_len,
    prefix_pool_keys,
    prefix_pool_values,
    page_table,
    root_len,
    mid_len,
    mid_parent,
    leaf_parent,
    residual,
    out_weight,
    post_gain,
    expert_ids,
    gate_weight,
    w_gate_up,
    w_down,
):
    vmem = pl.BlockSpec(memory_space=pltpu.VMEM)
    hbm = pl.BlockSpec(memory_space=pltpu.HBM)
    dma = lambda n: pltpu.SemaphoreType.DMA((n,))
    return pl.pallas_call(
        kernel,
        out_shape=(
            jax.ShapeDtypeStruct((TOKENS, 128), BF16),
            jax.ShapeDtypeStruct((16, 128), BF16),
        ),
        in_specs=[hbm] * 20,
        out_specs=(vmem, vmem),
        scratch_shapes=[
            pltpu.VMEM((1, 4096), BF16),
            pltpu.VMEM((1, 512), BF16),
            pltpu.VMEM((1, 512), BF16),
            pltpu.VMEM((1, 512), jnp.int32),
            pltpu.VMEM((1, TOKENS), jnp.int32),
            pltpu.VMEM((16, 128), BF16),
            pltpu.VMEM((TOKENS, 128), BF16),
            pltpu.VMEM((1, 128), F32),
            pltpu.VMEM((8, TOKENS), jnp.int32),
            pltpu.VMEM((8, TOKENS), F32),
            pltpu.SMEM((1,), jnp.int32),
            pltpu.SMEM((ROOTS,), jnp.int32),
            pltpu.SMEM((MIDS,), jnp.int32),
            pltpu.SMEM((MIDS,), jnp.int32),
            pltpu.VMEM((32, HEAD), F32),
            pltpu.VMEM((4, 8, HEAD), BF16),
            pltpu.VMEM((1, 512, 512), BF16),
            pltpu.VMEM((1, 512, 512), BF16),
            pltpu.VMEM((EXPERTS_HERE, 128, 2 * FFE), BF16),
            pltpu.VMEM((EXPERTS_HERE, FFE, 128), BF16),
            pltpu.VMEM((4, 2, 128, HEAD), BF16),
            pltpu.VMEM((4, 2, 128, HEAD), BF16),
            pltpu.VMEM((16, 128, HEAD), BF16),
            pltpu.VMEM((16, 128, 128), BF16),
            pltpu.VMEM((16, 128, HEAD), BF16),
            pltpu.VMEM((HEAD, 2048), BF16),
            pltpu.VMEM((TOKENS, 128), BF16),
            pltpu.VMEM((N, 64, 128), BF16),
            pltpu.VMEM((N, 8, HEAD), BF16),
            pltpu.VMEM((N, 64, HEAD), BF16),
            pltpu.VMEM((N, 80, 128), BF16),
            pltpu.VMEM((N, 80, 128), BF16),
            pltpu.VMEM((128, 128), F32),
            pltpu.VMEM((2, 32, 256), BF16),
            pltpu.VMEM((2, 32, 256), BF16),
            pltpu.VMEM((N, 8, 128), F32),
            pltpu.VMEM((N, 8, 128), F32),
            pltpu.VMEM((N, 32, 128), BF16),
            pltpu.VMEM((N, 16, 128), BF16),
            pltpu.VMEM((N, 16, 128), BF16),
            pltpu.VMEM((N, 16, 128), BF16),
            pltpu.VMEM((TOKENS, TOKENS), BF16),
            pltpu.VMEM((TOKENS, TOKENS), BF16),
            pltpu.VMEM((TOKENS, 128), F32),
            pltpu.VMEM((TOKENS, 256), BF16),
            pltpu.VMEM((N, 16, WIDE), BF16),
            pltpu.VMEM((N, 16, WIDE), BF16),
            pltpu.VMEM((N, 16, FFE), BF16),
            pltpu.VMEM((TOKENS, 256), BF16),
            pltpu.VMEM((N, 16, 128), BF16),
            pltpu.VMEM((N, 16, 128), BF16),
            dma(28),
            dma(2), dma(4),
            dma(2), dma(2),
            dma(1), dma(1),
            dma(1), dma(N),
            dma(1), dma(1),
            dma(4), dma(1),
            dma(1), dma(1),
            dma(1), dma(N),
            dma(1), dma(1),
            dma(1), dma(1),
            dma(1), dma(1),
            dma(1), dma(N),
            dma(1), dma(1),
        ],
        compiler_params=pltpu.CompilerParams(
            collective_id=0, has_side_effects=True
        ),
    )(
        fresh_queries,
        fresh_key,
        fresh_value,
        request_own_keys,
        request_own_values,
        leaf_len,
        prefix_pool_keys,
        prefix_pool_values,
        page_table.reshape(1, 512),
        root_len,
        mid_len,
        mid_parent,
        leaf_parent.reshape(1, TOKENS),
        residual,
        out_weight,
        post_gain.reshape(1, 128),
        expert_ids.T,
        gate_weight.T,
        w_gate_up,
        w_down,
    )


def solution(mesh):
    placed = (
        P(("row", "col"), None),
        P(("row", "col"), None),
        P(("row", "col"), None),
        P(("row", "col"), None, None),
        P(("row", "col"), None, None),
        P(("row", "col")),
        P(("row", "col"), None, None),
        P(("row", "col"), None, None),
        P(),
        P(),
        P(),
        P(),
        P(),
        P(None, "row"),
        P("col", "row"),
        P("row"),
        P(),
        P(),
        P("col", "row", None),
        P("col", None, "row"),
    )
    return jax.shard_map(
        per_device,
        mesh=mesh,
        in_specs=placed,
        out_specs=(P(None, "row"), P("col", "row")),
        check_vma=False,
    )
```
